512 devices in a mesh: mem: 8 (over z_lo, core), space: 64 (over z_hi, x, y).
Axes of the slice: x: 4, y: 8, z: 8 (z_hi: 2, z_lo: 4; z = z_hi * 4 + z_lo), core: 2. Of those that a mesh axis runs over, the one named last changes fastest.
Arguments:
- log_perm: float32 [128, 128, 2048], P('space', 'mem'), may hold values from -2 to 2
- concentration: float32 [128, 128, 2048], P('space', 'mem'), may hold values from -6 to 6
- well_cells: int32 [128], replicated, may hold values from 0 to 262143
- obs_data: float32 [128], replicated, may hold values from -6 to 6
- obs_var: float32 [128], replicated, may hold values from 0.05 to 0.5
- obs_noise: float32 [128, 128], P('mem'), may hold values from -6 to 6
Outputs:
- forecast: float32 [128, 128, 2048], P('space', 'mem')
- updated_log_perm: float32 [128, 128, 2048], P('space', 'mem')
The draws below stay inside these ranges and needn't reach their ends.
Inputs may be any that keep to these rules, and one draw needn't show every extreme that they name: `well_cells`: cells flattened as row times 2048 plus column.
All inputs are finite; a program needn't handle non-finite values.
Results may differ from the reference program's by a relative error of at most 0.0034.
Values may be sent and summed in bfloat16 or wider, within the bound.
No kernel may reach another device: no remote copies, remote signals or barrier semaphores. Data moves between devices by JAX's collectives and lax.ppermute only.
A program may use at most 128 MiB of HBM per device.

```python
import math
import jax
import jax.numpy as jnp
from jax import lax

NY = 2048
NOBS = 128
MEMBERS = 128
NX = 128


def plant(values, key, low, high):
    longest = values.shape.index(max(values.shape))
    spots = []
    for shift in (0, 1):
        where = [jax.random.randint(jax.random.fold_in(key, axis), (), 0, length) for axis, length in enumerate(values.shape)]
        where[longest] = (where[longest] + shift) % values.shape[longest]
        spots.append(tuple(where))
    return values.at[spots[0]].set(low).at[spots[1]].set(high)


def shard_levels(rng, extent, cuts, low, top_value):
    factor_of, own = 1.0, jax.random.fold_in(rng, 6)
    for dim, blocks in cuts:
        steps = jnp.exp(jax.random.uniform(jax.random.fold_in(own, dim), (blocks,), jnp.float32, low / len(cuts), top_value / len(cuts)))
        factor_of = factor_of * jnp.repeat(steps, extent[dim] // blocks).reshape([-1 if axis == dim else 1 for axis in range(len(extent))])
    return factor_of


def normal_values(rng, extent, scale, bound, cuts=(), kind=jnp.bfloat16):
    gain = shard_levels(rng, extent, cuts, -0.22, 0.18) if cuts else 1.0
    array = jax.random.normal(rng, extent, jnp.float32) * scale * gain
    return jnp.minimum(jnp.maximum(array, -bound), bound).astype(kind)


def setup_inputs(seed: int = 0) -> dict:
    key_of = jax.random.split(jax.random.key(seed), 7)
    log_perm = normal_values(key_of[0], (NX, MEMBERS, NY), 0.5, 2.0, ((0, 64), (1, 8)), jnp.float32)
    concentration = normal_values(key_of[1], (NX, MEMBERS, NY), 1.0, 6.0, ((0, 64), (1, 8)), jnp.float32)
    well_cells = plant(jax.random.randint(key_of[2], (NOBS,), 0, NX * NY), jax.random.fold_in(key_of[2], 1), 0, (NX * NY) - 1).astype(jnp.int32)
    obs_data = normal_values(key_of[3], (NOBS,), 1.0, 6.0, (), jnp.float32)
    obs_var = jnp.clip(jnp.exp(jax.random.uniform(key_of[4], (NOBS,), jnp.float32, math.log(0.05), math.log(0.5))), 0.05, 0.5)
    obs_noise = normal_values(key_of[5], (MEMBERS, NOBS), 1.0, 6.0, ((0, 8),), jnp.float32)
    return dict(log_perm=log_perm, concentration=concentration, well_cells=well_cells, obs_data=obs_data, obs_var=obs_var, obs_noise=obs_noise)


time_step = 0.03
inflation = 4.0

def advance(conc_ext, conduct_ext):
    conc_pad = jnp.pad(conc_ext, ((0, 0), (0, 0), (1, 1)))
    cond_pad = jnp.pad(conduct_ext, ((0, 0), (0, 0), (1, 1)))
    centre = conc_pad[1:-1, :, 1:-1]
    centre_cond = cond_pad[1:-1, :, 1:-1]
    inflow = jnp.zeros_like(centre)
    sides = ((conc_pad[:-2, :, 1:-1], cond_pad[:-2, :, 1:-1]), (conc_pad[2:, :, 1:-1], cond_pad[2:, :, 1:-1]), (conc_pad[1:-1, :, :-2], cond_pad[1:-1, :, :-2]), (conc_pad[1:-1, :, 2:], cond_pad[1:-1, :, 2:]))
    for conc_side, cond_side in sides:
        inflow = inflow + 0.5 * (centre_cond + cond_side) * (conc_side - centre)
    return centre + time_step * inflow

def cholesky_solve(matrix, target):
    factor = jnp.linalg.cholesky(matrix)
    middle = lax.linalg.triangular_solve(factor, target, left_side=True, lower=True)
    return lax.linalg.triangular_solve(factor, middle, left_side=True, lower=True, transpose_a=True)

def transform(predicted, noise_all, obs_data, obs_var):
    members = predicted.shape[0]
    anomaly = predicted - lax.optimization_barrier(jnp.mean(predicted, axis=0, keepdims=True))
    covariance = jnp.dot(anomaly.T.astype(jnp.float32), anomaly.astype(jnp.float32), precision=lax.Precision.HIGHEST, preferred_element_type=jnp.float32) / (members - 1) + inflation * jnp.diag(obs_var)
    innovation = obs_data[None, :] + jnp.sqrt(inflation * obs_var)[None, :] * noise_all - predicted
    solved = cholesky_solve(covariance, innovation.T)
    weights = jnp.dot(anomaly.astype(jnp.float32), solved.astype(jnp.float32), precision=lax.Precision.HIGHEST, preferred_element_type=jnp.float32) / (members - 1)
    centred = weights - lax.optimization_barrier(jnp.mean(weights, axis=0, keepdims=True))
    return centred.astype(jnp.bfloat16)

def reference(log_perm, concentration, well_cells, obs_data, obs_var, obs_noise):
    conduct = jnp.exp(log_perm)
    conduct_ext = jnp.pad(conduct, ((1, 1), (0, 0), (0, 0)))
    tracer = concentration
    for repeat in range(2):
        tracer = advance(jnp.pad(tracer, ((1, 1), (0, 0), (0, 0))), conduct_ext)
    predicted = tracer[well_cells // NY, :, well_cells % NY].T
    centred = transform(predicted, obs_noise, obs_data, obs_var)
    perm_low = log_perm.astype(jnp.bfloat16)
    increment = jnp.einsum('xiy,ij->xjy', perm_low.astype(jnp.float32), centred.astype(jnp.float32), precision=lax.Precision.HIGHEST)
    return (tracer, log_perm + increment)
```

```python
import jax
import jax.numpy as jnp
from jax import lax
from jax.experimental import pallas as pl
from jax.experimental.pallas import tpu as pltpu
from jax.sharding import Mesh, PartitionSpec as P

F32, BF16 = jnp.float32, jnp.bfloat16
time_step = 0.03
inflation = 4.0
HIGH = lax.Precision.HIGHEST
TN = (((0,), (0,)), ((), ()))
PANEL = 16
MEM = ("z_lo", "core")
SPACE = ("z_hi", "x", "y")
ORDER = (0, 2, 4, 6, 1, 3, 5, 7)
VMEM_LIMIT = 48 * 1024 * 1024

def split3(x):
    hi = x.astype(BF16)
    rest = x - hi.astype(F32)
    mid = rest.astype(BF16)
    low = (rest - mid.astype(F32)).astype(BF16)
    return hi, mid, low


def factor_panel(rows, base):
    height = rows.shape[0]
    index = lax.broadcasted_iota(jnp.int32, (height, 128), 0)
    lanes = rows.shape[1] // 128
    cols = [jnp.broadcast_to(rows[:, base + c : base + c + 1], (height, 128)) for c in range(height)]
    tiles = [rows[:, t * 128 : (t + 1) * 128] for t in range(lanes)]
    for k in range(height):
        scale = lax.rsqrt(cols[k][k : k + 1, :])
        below = cols[k] * scale
        masked = jnp.where(index > k, below, 0.0)
        for c in range(k + 1, height):
            cols[c] = cols[c] - masked * below[c : c + 1, :]
        for t in range(lanes):
            top = tiles[t][k : k + 1, :] * scale
            tiles[t] = jnp.where(index == k, top, tiles[t] - masked * top)
    return jnp.concatenate(tiles, axis=1)


def weights_of(pred, own_noise, obs_data, obs_var, work, solved):
    members = pred.shape[0]
    anomaly = pred - jnp.mean(pred, axis=0, keepdims=True)
    innovation = obs_data + jnp.sqrt(inflation * obs_var) * own_noise - pred[:16]
    cov = lax.dot_general(anomaly, anomaly, TN, precision=HIGH, preferred_element_type=F32) / (members - 1)
    r = lax.broadcasted_iota(jnp.int32, (128, 128), 0)
    c = lax.broadcasted_iota(jnp.int32, (128, 128), 1)
    cov = cov + jnp.where(r == c, jnp.broadcast_to(inflation * obs_var, (128, 128)), 0.0)
    work[:, 0:128] = cov
    work[:, 128:256] = anomaly.T
    padded = jnp.concatenate([innovation, jnp.zeros((112, 128), F32)], axis=0)
    work[:, 256:384] = padded.T
    for p in range(128 // PANEL):
        u = factor_panel(work[p * PANEL : (p + 1) * PANEL, :], p * PANEL)
        solved[p * PANEL : (p + 1) * PANEL, :] = u[:, 128:384]
        if p < 128 // PANEL - 1:
            h, m, l = split3(u)
            left = jnp.concatenate([h, h, m, h, l, m], axis=0)[:, 0:128]
            right = jnp.concatenate([h, m, h, l, h, m], axis=0)
            update = lax.dot_general(left, right, TN, preferred_element_type=F32)
            work[(p + 1) * PANEL :, :] = work[(p + 1) * PANEL :, :] - update[(p + 1) * PANEL :, :]
    w = lax.dot_general(
        solved[:, 128:256], solved[:, 0:128], TN, precision=HIGH, preferred_element_type=F32
    )[:16] / (members - 1)
    return w - jnp.mean(w, axis=1, keepdims=True)


def along_row(conc, link, left_edge):
    width = conc.shape[1]
    lane = lax.broadcasted_iota(jnp.int32, conc.shape, 1)
    right = jnp.where(lane == width - 1, 0.0, pltpu.roll(conc, width - 1, 1))
    flux = link * (right - conc)
    from_left = jnp.where(lane == 0, left_edge * conc, pltpu.roll(flux, 1, 1))
    return flux - from_left


def link_right(conduct):
    width = conduct.shape[1]
    lane = lax.broadcasted_iota(jnp.int32, conduct.shape, 1)
    return 0.5 * (conduct + jnp.where(lane == width - 1, 0.0, pltpu.roll(conduct, width - 1, 1)))


def prepare_kernel(perm_ref, conc_ref, up_ref, down_ref, low_ref, part_ref, conduct_ref):
    perm0, perm1 = perm_ref[0], perm_ref[1]
    conc0, conc1 = conc_ref[0], conc_ref[1]
    low_ref[0], low_ref[1] = perm0.astype(BF16), perm1.astype(BF16)
    cond0, cond1 = jnp.exp(perm0), jnp.exp(perm1)
    conduct_ref[0], conduct_ref[1] = cond0, cond1
    between = 0.5 * (cond0 + cond1) * (conc1 - conc0)
    part0 = conc0 + time_step * (along_row(conc0, link_right(cond0), 0.5 * cond0) + between)
    part1 = conc1 + time_step * (along_row(conc1, link_right(cond1), 0.5 * cond1) - between)
    part_ref[0], part_ref[1] = part0, part1
    down_ref[0], down_ref[1], down_ref[2] = conc0.astype(BF16), cond0.astype(BF16), part0.astype(BF16)
    up_ref[0], up_ref[1], up_ref[2] = conc1.astype(BF16), cond1.astype(BF16), part1.astype(BF16)


def prepare(log_perm, conc):
    rows, members, width = log_perm.shape
    edge = jax.ShapeDtypeStruct((3, members, width), BF16)
    full = jax.ShapeDtypeStruct(log_perm.shape, F32)
    return pl.pallas_call(
        prepare_kernel,
        out_shape=(edge, edge, jax.ShapeDtypeStruct(log_perm.shape, BF16), full, full),
        cost_estimate=pl.CostEstimate(flops=2_000_000, bytes_accessed=1_600_000, transcendentals=65536),
        compiler_params=pltpu.CompilerParams(vmem_limit_bytes=VMEM_LIMIT),
        name="prepare",
    )(log_perm, conc)


def advance_kernel(place_ref, conc_ref, conduct_ref, part_ref, above_ref, below_ref, wells_ref, out_ref, picked_ref):
    strip = place_ref[0]
    conc0, conc1 = conc_ref[0], conc_ref[1]
    cond0, cond1 = conduct_ref[0], conduct_ref[1]
    conc_a, cond_a, part_a = [above_ref[i].astype(F32) for i in range(3)]
    conc_b, cond_b, part_b = [below_ref[i].astype(F32) for i in range(3)]
    link_a = 0.5 * (cond0 + cond_a)
    link_b = 0.5 * (cond1 + cond_b)
    gain_a = time_step * (link_a * (conc_a - conc0))
    gain_b = time_step * (link_b * (conc_b - conc1))
    once0, once1 = part_ref[0] + gain_a, part_ref[1] + gain_b
    once_a = jnp.where(strip == 0, 0.0, part_a - gain_a)
    once_b = jnp.where(strip == STRIPS - 1, 0.0, part_b - gain_b)
    between = 0.5 * (cond0 + cond1) * (once1 - once0)
    twice0 = once0 + time_step * (
        along_row(once0, link_right(cond0), 0.5 * cond0) + between + link_a * (once_a - once0)
    )
    twice1 = once1 + time_step * (
        along_row(once1, link_right(cond1), 0.5 * cond1) - between + link_b * (once_b - once1)
    )
    out_ref[0], out_ref[1] = twice0, twice1
    members, width = twice0.shape
    chunk = 256
    total = jnp.zeros((3 * members, 128), F32)
    for row, values in enumerate((twice0, twice1)):
        pieces = jnp.concatenate(split3(values), axis=0)
        column = wells_ref[...] - (2 * strip + row) * width
        for start in range(0, width, chunk):
            here = lax.broadcasted_iota(jnp.int32, (chunk, 128), 0) + start
            chosen = jnp.where(here == column, 1.0, 0.0).astype(BF16)
            total = total + jnp.dot(pieces[:, start : start + chunk], chosen, preferred_element_type=F32)
    picked = total[:members] + total[members : 2 * members] + total[2 * members :]
    for copy in range(picked_ref.shape[0]):
        picked_ref[copy] = picked


def advance(place, conc, conduct, part, above, below, wells, copies):
    vmem = pl.BlockSpec(memory_space=pltpu.VMEM)
    return pl.pallas_call(
        advance_kernel,
        out_shape=(
            jax.ShapeDtypeStruct(conc.shape, F32),
            jax.ShapeDtypeStruct((copies, conc.shape[1], 128), F32),
        ),
        in_specs=[pl.BlockSpec(memory_space=pltpu.SMEM)] + [vmem] * 6,
        out_specs=(vmem, vmem),
        cost_estimate=pl.CostEstimate(flops=60_000_000, bytes_accessed=1_800_000, transcendentals=0),
        compiler_params=pltpu.CompilerParams(vmem_limit_bytes=VMEM_LIMIT),
        name="advance",
    )(place, conc, conduct, part, above, below, wells)


def update_kernel(place_ref, found_ref, noise_ref, data_ref, var_ref, perm_ref, even_ref, odd_ref, out_ref, pred, work, solved, low, sem):
    group = place_ref[1]
    copies = []
    for position in range(8):
        source = (even_ref if position < 4 else odd_ref).at[position % 4]
        for row in range(2):
            copies.append(
                pltpu.make_async_copy(source.at[row], low.at[row, pl.ds(position * 16, 16)], sem.at[position, row])
            )
    for copy in copies:
        copy.start()
    for position, flip in enumerate(ORDER):
        block = lax.bitwise_xor(group, flip)
        pred[pl.ds(position * 16, 16), :] = found_ref[2 * block] + found_ref[2 * block + 1]
    centred = weights_of(pred[...], noise_ref[...], data_ref[...], var_ref[...], work, solved).astype(BF16)
    for copy in copies:
        copy.wait()
    for row in range(2):
        out_ref[row] = perm_ref[row] + jnp.dot(centred, low[row], preferred_element_type=F32)


def update(place, found, noise, obs_data, obs_var, log_perm, even, odd):
    vmem = pl.BlockSpec(memory_space=pltpu.VMEM)
    anywhere = pl.BlockSpec(memory_space=pl.ANY)
    rows, members, width = log_perm.shape
    return pl.pallas_call(
        update_kernel,
        out_shape=jax.ShapeDtypeStruct(log_perm.shape, F32),
        in_specs=[pl.BlockSpec(memory_space=pltpu.SMEM)] + [vmem] * 5 + [anywhere] * 2,
        out_specs=vmem,
        scratch_shapes=[
            pltpu.VMEM((128, 128), F32),
            pltpu.VMEM((128, 384), F32),
            pltpu.VMEM((128, 256), F32),
            pltpu.VMEM((rows, 128, width), BF16),
            pltpu.SemaphoreType.DMA((8, 2)),
        ],
        cost_estimate=pl.CostEstimate(flops=200_000_000, bytes_accessed=1_700_000, transcendentals=128),
        compiler_params=pltpu.CompilerParams(vmem_limit_bytes=VMEM_LIMIT),
        name="update",
    )(place, found, noise, obs_data, obs_var, log_perm, even, odd)


STRIPS = 64


def shifted(value, shift):
    pairs = [(i, i + shift) for i in range(STRIPS) if 0 <= i + shift < STRIPS]
    return lax.ppermute(value, SPACE, pairs)


def swapped(value, axis, flip):
    return lax.ppermute(value, axis, [(i, i ^ flip) for i in range(lax.axis_size(axis))])


def local(log_perm, concentration, well_cells, obs_data, obs_var, obs_noise):
    place = jnp.stack([lax.axis_index(SPACE), lax.axis_index(MEM)]).astype(jnp.int32)
    up, down, low, part, conduct = prepare(log_perm, concentration)
    above, below = shifted(up, 1), shifted(down, -1)
    two = jnp.stack([low, swapped(low, "z_lo", 1)])
    even = jnp.concatenate([two, swapped(two, "z_lo", 2)])
    odd = swapped(even, "core", 1)
    tracer, picked = advance(place, concentration, conduct, part, above, below, well_cells[None], 32)
    found = lax.all_to_all(picked, ("x", "y"), 0, 0, tiled=True)
    found = jnp.broadcast_to(jnp.sum(found, axis=0)[None], (16, 16, 128))
    found = lax.all_to_all(found, ("z_lo", "core", "z_hi"), 0, 0, tiled=True)
    updated = update(place, found, obs_noise, obs_data[None], obs_var[None], log_perm, even, odd)
    return (tracer, updated)


def solution(mesh):
    fine = Mesh(mesh.devices.reshape(4, 2, 2, 4, 8), MEM + SPACE)
    return jax.shard_map(
        local,
        mesh=fine,
        in_specs=(P(SPACE, MEM, None), P(SPACE, MEM, None), P(), P(), P(), P(MEM, None)),
        out_specs=(P(SPACE, MEM, None), P(SPACE, MEM, None)),
        check_vma=False,
    )
```

```python
import jax
import jax.numpy as jnp
from jax import lax
from jax.experimental import pallas as pl
from jax.experimental.pallas import tpu as pltpu
from jax.sharding import Mesh, PartitionSpec as P

F32, BF16 = jnp.float32, jnp.bfloat16
time_step = 0.03
inflation = 4.0
HIGH = lax.Precision.HIGHEST
TN = (((0,), (0,)), ((), ()))
PANEL = 16
MEM = ("z_lo", "core")
SPACE = ("z_hi", "x", "y")
ORDER = (0, 2, 4, 6, 1, 3, 5, 7)
VMEM_LIMIT = 48 * 1024 * 1024

def split3(x):
    hi = x.astype(BF16)
    rest = x - hi.astype(F32)
    mid = rest.astype(BF16)
    low = (rest - mid.astype(F32)).astype(BF16)
    return hi, mid, low


def factor_panel(rows, base):
    height = rows.shape[0]
    index = lax.broadcasted_iota(jnp.int32, (height, 128), 0)
    lanes = rows.shape[1] // 128
    cols = [jnp.broadcast_to(rows[:, base + c : base + c + 1], (height, 128)) for c in range(height)]
    tiles = [rows[:, t * 128 : (t + 1) * 128] for t in range(lanes)]
    for k in range(height):
        scale = lax.rsqrt(cols[k][k : k + 1, :])
        below = cols[k] * scale
        masked = jnp.where(index > k, below, 0.0)
        for c in range(k + 1, height):
            cols[c] = cols[c] - masked * below[c : c + 1, :]
        for t in range(lanes):
            top = tiles[t][k : k + 1, :] * scale
            tiles[t] = jnp.where(index == k, top, tiles[t] - masked * top)
    return jnp.concatenate(tiles, axis=1)


def weights_of(pred, own_noise, obs_data, obs_var, work, solved):
    members = pred.shape[0]
    anomaly = pred - jnp.mean(pred, axis=0, keepdims=True)
    innovation = obs_data + jnp.sqrt(inflation * obs_var) * own_noise - pred[:16]
    cov = lax.dot_general(anomaly, anomaly, TN, precision=HIGH, preferred_element_type=F32) / (members - 1)
    r = lax.broadcasted_iota(jnp.int32, (128, 128), 0)
    c = lax.broadcasted_iota(jnp.int32, (128, 128), 1)
    cov = cov + jnp.where(r == c, jnp.broadcast_to(inflation * obs_var, (128, 128)), 0.0)
    work[:, 0:128] = cov
    work[:, 128:256] = anomaly.T
    padded = jnp.concatenate([innovation, jnp.zeros((112, 128), F32)], axis=0)
    work[:, 256:384] = padded.T
    for p in range(128 // PANEL):
        u = factor_panel(work[p * PANEL : (p + 1) * PANEL, :], p * PANEL)
        solved[p * PANEL : (p + 1) * PANEL, :] = u[:, 128:384]
        if p < 128 // PANEL - 1:
            h, m, l = split3(u)
            left = jnp.concatenate([h, h, m, h, l, m], axis=0)[:, 0:128]
            right = jnp.concatenate([h, m, h, l, h, m], axis=0)
            update = lax.dot_general(left, right, TN, preferred_element_type=F32)
            work[(p + 1) * PANEL :, :] = work[(p + 1) * PANEL :, :] - update[(p + 1) * PANEL :, :]
    w = lax.dot_general(
        solved[:, 128:256], solved[:, 0:128], TN, precision=HIGH, preferred_element_type=F32
    )[:16] / (members - 1)
    return w - jnp.mean(w, axis=1, keepdims=True)


def along_row(conc, link, left_edge):
    width = conc.shape[1]
    lane = lax.broadcasted_iota(jnp.int32, conc.shape, 1)
    right = jnp.where(lane == width - 1, 0.0, pltpu.roll(conc, width - 1, 1))
    flux = link * (right - conc)
    from_left = jnp.where(lane == 0, left_edge * conc, pltpu.roll(flux, 1, 1))
    return flux - from_left


def link_right(conduct):
    width = conduct.shape[1]
    lane = lax.broadcasted_iota(jnp.int32, conduct.shape, 1)
    return 0.5 * (conduct + jnp.where(lane == width - 1, 0.0, pltpu.roll(conduct, width - 1, 1)))


def prepare_kernel(
    perm_hbm, conc_hbm, wells_hbm, data_hbm, var_hbm, noise_hbm,
    up_ref, down_ref, low_ref, part_ref, conduct_ref, wells_ref, data_ref, var_ref, noise_ref,
    perm_ref, conc_ref, sem,
):
    main = [
        pltpu.make_async_copy(source.at[row], target.at[row], sem.at[2 * i + row])
        for i, (source, target) in enumerate(((perm_hbm, perm_ref), (conc_hbm, conc_ref)))
        for row in range(2)
    ]
    small = [
        pltpu.make_async_copy(source, target, sem.at[4 + i])
        for i, (source, target) in enumerate(
            ((wells_hbm, wells_ref), (data_hbm, data_ref), (var_hbm, var_ref), (noise_hbm, noise_ref))
        )
    ]
    for copy in main + small:
        copy.start()
    for copy in main:
        copy.wait()
    perm0, perm1 = perm_ref[0], perm_ref[1]
    conc0, conc1 = conc_ref[0], conc_ref[1]
    low_ref[0], low_ref[1] = perm0.astype(BF16), perm1.astype(BF16)
    cond0, cond1 = jnp.exp(perm0), jnp.exp(perm1)
    conduct_ref[0], conduct_ref[1] = cond0, cond1
    between = 0.5 * (cond0 + cond1) * (conc1 - conc0)
    part0 = conc0 + time_step * (along_row(conc0, link_right(cond0), 0.5 * cond0) + between)
    part1 = conc1 + time_step * (along_row(conc1, link_right(cond1), 0.5 * cond1) - between)
    part_ref[0], part_ref[1] = part0, part1
    down_ref[0], down_ref[1], down_ref[2] = conc0.astype(BF16), cond0.astype(BF16), part0.astype(BF16)
    up_ref[0], up_ref[1], up_ref[2] = conc1.astype(BF16), cond1.astype(BF16), part1.astype(BF16)
    for copy in small:
        copy.wait()


def prepare(log_perm, conc, wells, obs_data, obs_var, noise):
    rows, members, width = log_perm.shape
    edge = jax.ShapeDtypeStruct((3, members, width), BF16)
    full = jax.ShapeDtypeStruct(log_perm.shape, F32)
    small = [jax.ShapeDtypeStruct(a.shape, a.dtype) for a in (wells, obs_data, obs_var, noise)]
    return pl.pallas_call(
        prepare_kernel,
        out_shape=(edge, edge, jax.ShapeDtypeStruct(log_perm.shape, BF16), full, full, *small),
        in_specs=[pl.BlockSpec(memory_space=pltpu.HBM)] * 6,
        out_specs=[pl.BlockSpec(memory_space=pltpu.VMEM)] * 9,
        scratch_shapes=[
            pltpu.VMEM(log_perm.shape, F32),
            pltpu.VMEM(log_perm.shape, F32),
            pltpu.SemaphoreType.DMA((8,)),
        ],
        cost_estimate=pl.CostEstimate(flops=2_000_000, bytes_accessed=1_600_000, transcendentals=65536),
        compiler_params=pltpu.CompilerParams(vmem_limit_bytes=VMEM_LIMIT),
        name="prepare",
    )(*[pltpu.with_memory_space_constraint(a, pltpu.HBM) for a in (log_perm, conc, wells, obs_data, obs_var, noise)])


def spread_kernel(found_ref, out_ref):
    total = found_ref[0]
    for i in range(1, found_ref.shape[0]):
        total = total + found_ref[i]
    for copy in range(out_ref.shape[0]):
        out_ref[copy] = total


def spread(found, copies):
    return pl.pallas_call(
        spread_kernel,
        out_shape=jax.ShapeDtypeStruct((copies, *found.shape[1:]), F32),
        cost_estimate=pl.CostEstimate(flops=65536, bytes_accessed=400_000, transcendentals=0),
        compiler_params=pltpu.CompilerParams(vmem_limit_bytes=VMEM_LIMIT),
        name="spread",
    )(found)


def advance_kernel(place_ref, conc_ref, conduct_ref, part_ref, above_ref, below_ref, wells_ref, out_ref, picked_ref):
    strip = place_ref[0]
    conc0, conc1 = conc_ref[0], conc_ref[1]
    cond0, cond1 = conduct_ref[0], conduct_ref[1]
    conc_a, cond_a, part_a = [above_ref[i].astype(F32) for i in range(3)]
    conc_b, cond_b, part_b = [below_ref[i].astype(F32) for i in range(3)]
    link_a = 0.5 * (cond0 + cond_a)
    link_b = 0.5 * (cond1 + cond_b)
    gain_a = time_step * (link_a * (conc_a - conc0))
    gain_b = time_step * (link_b * (conc_b - conc1))
    once0, once1 = part_ref[0] + gain_a, part_ref[1] + gain_b
    once_a = jnp.where(strip == 0, 0.0, part_a - gain_a)
    once_b = jnp.where(strip == STRIPS - 1, 0.0, part_b - gain_b)
    between = 0.5 * (cond0 + cond1) * (once1 - once0)
    twice0 = once0 + time_step * (
        along_row(once0, link_right(cond0), 0.5 * cond0) + between + link_a * (once_a - once0)
    )
    twice1 = once1 + time_step * (
        along_row(once1, link_right(cond1), 0.5 * cond1) - between + link_b * (once_b - once1)
    )
    out_ref[0], out_ref[1] = twice0, twice1
    members, width = twice0.shape
    chunk = 256
    total = jnp.zeros((3 * members, 128), F32)
    for row, values in enumerate((twice0, twice1)):
        pieces = jnp.concatenate(split3(values), axis=0)
        column = wells_ref[...] - (2 * strip + row) * width
        for start in range(0, width, chunk):
            here = lax.broadcasted_iota(jnp.int32, (chunk, 128), 0) + start
            chosen = jnp.where(here == column, 1.0, 0.0).astype(BF16)
            total = total + jnp.dot(pieces[:, start : start + chunk], chosen, preferred_element_type=F32)
    picked = total[:members] + total[members : 2 * members] + total[2 * members :]
    for copy in range(picked_ref.shape[0]):
        picked_ref[copy] = picked


def advance(place, conc, conduct, part, above, below, wells, copies):
    vmem = pl.BlockSpec(memory_space=pltpu.VMEM)
    return pl.pallas_call(
        advance_kernel,
        out_shape=(
            jax.ShapeDtypeStruct(conc.shape, F32),
            jax.ShapeDtypeStruct((copies, conc.shape[1], 128), F32),
        ),
        in_specs=[pl.BlockSpec(memory_space=pltpu.SMEM)] + [vmem] * 6,
        out_specs=(vmem, vmem),
        cost_estimate=pl.CostEstimate(flops=60_000_000, bytes_accessed=1_800_000, transcendentals=0),
        compiler_params=pltpu.CompilerParams(vmem_limit_bytes=VMEM_LIMIT),
        name="advance",
    )(place, conc, conduct, part, above, below, wells)


def update_kernel(place_ref, found_ref, noise_ref, data_ref, var_ref, perm_ref, even_ref, odd_ref, out_ref, pred, work, solved, low, sem):
    group = place_ref[1]
    copies = []
    for position in range(8):
        source = (even_ref if position < 4 else odd_ref).at[position % 4]
        for row in range(2):
            copies.append(
                pltpu.make_async_copy(source.at[row], low.at[row, pl.ds(position * 16, 16)], sem.at[position, row])
            )
    for copy in copies:
        copy.start()
    for position, flip in enumerate(ORDER):
        block = lax.bitwise_xor(group, flip)
        pred[pl.ds(position * 16, 16), :] = found_ref[2 * block] + found_ref[2 * block + 1]
    centred = weights_of(pred[...], noise_ref[...], data_ref[...], var_ref[...], work, solved).astype(BF16)
    for copy in copies:
        copy.wait()
    for row in range(2):
        out_ref[row] = perm_ref[row] + jnp.dot(centred, low[row], preferred_element_type=F32)


def update(place, found, noise, obs_data, obs_var, log_perm, even, odd):
    vmem = pl.BlockSpec(memory_space=pltpu.VMEM)
    anywhere = pl.BlockSpec(memory_space=pl.ANY)
    rows, members, width = log_perm.shape
    return pl.pallas_call(
        update_kernel,
        out_shape=jax.ShapeDtypeStruct(log_perm.shape, F32),
        in_specs=[pl.BlockSpec(memory_space=pltpu.SMEM)] + [vmem] * 5 + [anywhere] * 2,
        out_specs=vmem,
        scratch_shapes=[
            pltpu.VMEM((128, 128), F32),
            pltpu.VMEM((128, 384), F32),
            pltpu.VMEM((128, 256), F32),
            pltpu.VMEM((rows, 128, width), BF16),
            pltpu.SemaphoreType.DMA((8, 2)),
        ],
        cost_estimate=pl.CostEstimate(flops=200_000_000, bytes_accessed=1_700_000, transcendentals=128),
        compiler_params=pltpu.CompilerParams(vmem_limit_bytes=VMEM_LIMIT),
        name="update",
    )(place, found, noise, obs_data, obs_var, log_perm, even, odd)


STRIPS = 64


def shifted(value, shift):
    pairs = [(i, i + shift) for i in range(STRIPS) if 0 <= i + shift < STRIPS]
    return lax.ppermute(value, SPACE, pairs)


def swapped(value, axis, flip):
    return lax.ppermute(value, axis, [(i, i ^ flip) for i in range(lax.axis_size(axis))])


def local(log_perm, concentration, well_cells, obs_data, obs_var, obs_noise):
    place = jnp.stack([lax.axis_index(SPACE), lax.axis_index(MEM)]).astype(jnp.int32)
    up, down, low, part, conduct, wells, data, var, noise = prepare(
        log_perm, concentration, well_cells[None], obs_data[None], obs_var[None], obs_noise
    )
    above, below = shifted(up, 1), shifted(down, -1)
    tracer, picked = advance(place, concentration, conduct, part, above, below, wells, 32)
    low, picked = lax.optimization_barrier((low, picked))
    found = lax.all_to_all(picked, ("x", "y"), 0, 0, tiled=True)
    even = jnp.stack([low] + [swapped(low, "z_lo", flip) for flip in (1, 2, 3)])
    even, found = lax.optimization_barrier((even, found))
    found = lax.all_to_all(spread(found, 16), ("z_lo", "core", "z_hi"), 0, 0, tiled=True)
    odd = swapped(even, "core", 1)
    updated = update(place, found, noise, data, var, log_perm, even, odd)
    return (tracer, updated)


def solution(mesh):
    fine = Mesh(mesh.devices.reshape(4, 2, 2, 4, 8), MEM + SPACE)
    return jax.shard_map(
        local,
        mesh=fine,
        in_specs=(P(SPACE, MEM, None), P(SPACE, MEM, None), P(), P(), P(), P(MEM, None)),
        out_specs=(P(SPACE, MEM, None), P(SPACE, MEM, None)),
        check_vma=False,
    )
```

```python
import functools

import jax
import jax.numpy as jnp
from jax import lax
from jax.experimental import pallas as pl
from jax.experimental.pallas import tpu as pltpu
from jax.sharding import Mesh, PartitionSpec as P

F32, BF16 = jnp.float32, jnp.bfloat16
time_step = 0.03
inflation = 4.0
HIGH = lax.Precision.HIGHEST
TN = (((0,), (0,)), ((), ()))
PANEL = 16
MEM = ("z_lo", "core")
SPACE = ("z_hi", "x", "y")
SENT = ((1, 0), (1, 1), (1, 2), (0, 0), (0, 1), (2, 0), (2, 1))
VMEM_LIMIT = 48 * 1024 * 1024

def split3(x):
    hi = x.astype(BF16)
    rest = x - hi.astype(F32)
    mid = rest.astype(BF16)
    low = (rest - mid.astype(F32)).astype(BF16)
    return hi, mid, low


def factor_panel(rows, base):
    height = rows.shape[0]
    index = lax.broadcasted_iota(jnp.int32, (height, 128), 0)
    lanes = rows.shape[1] // 128
    cols = [jnp.broadcast_to(rows[:, base + c : base + c + 1], (height, 128)) for c in range(height)]
    tiles = [rows[:, t * 128 : (t + 1) * 128] for t in range(lanes)]
    for k in range(height):
        scale = lax.rsqrt(cols[k][k : k + 1, :])
        below = cols[k] * scale
        masked = jnp.where(index > k, below, 0.0)
        for c in range(k + 1, height):
            cols[c] = cols[c] - masked * below[c : c + 1, :]
        for t in range(lanes):
            top = tiles[t][k : k + 1, :] * scale
            tiles[t] = jnp.where(index == k, top, tiles[t] - masked * top)
    return jnp.concatenate(tiles, axis=1)


def weights_of(pred, own, own_noise, obs_data, obs_var, work, solved):
    members = pred.shape[0]
    anomaly = pred - jnp.mean(pred, axis=0, keepdims=True)
    innovation = obs_data + jnp.sqrt(inflation * obs_var) * own_noise - own
    cov = lax.dot_general(anomaly, anomaly, TN, precision=HIGH, preferred_element_type=F32) / (members - 1)
    r = lax.broadcasted_iota(jnp.int32, (128, 128), 0)
    c = lax.broadcasted_iota(jnp.int32, (128, 128), 1)
    cov = cov + jnp.where(r == c, jnp.broadcast_to(inflation * obs_var, (128, 128)), 0.0)
    work[:, 0:128] = cov
    work[:, 128:256] = anomaly.T
    padded = jnp.concatenate([innovation, jnp.zeros((112, 128), F32)], axis=0)
    work[:, 256:384] = padded.T
    for p in range(128 // PANEL):
        u = factor_panel(work[p * PANEL : (p + 1) * PANEL, :], p * PANEL)
        solved[p * PANEL : (p + 1) * PANEL, :] = u[:, 128:384]
        if p < 128 // PANEL - 1:
            h, m, l = split3(u)
            left = jnp.concatenate([h, h, m, h, l, m], axis=0)[:, 0:128]
            right = jnp.concatenate([h, m, h, l, h, m], axis=0)
            update = lax.dot_general(left, right, TN, preferred_element_type=F32)
            work[(p + 1) * PANEL :, :] = work[(p + 1) * PANEL :, :] - update[(p + 1) * PANEL :, :]
    w = lax.dot_general(
        solved[:, 128:256], solved[:, 0:128], TN, precision=HIGH, preferred_element_type=F32
    )[:16] / (members - 1)
    return w - jnp.mean(w, axis=1, keepdims=True)


def along_row(conc, link, left_edge):
    width = conc.shape[1]
    lane = lax.broadcasted_iota(jnp.int32, conc.shape, 1)
    right = jnp.where(lane == width - 1, 0.0, pltpu.roll(conc, width - 1, 1))
    flux = link * (right - conc)
    from_left = jnp.where(lane == 0, left_edge * conc, pltpu.roll(flux, 1, 1))
    return flux - from_left


def link_right(conduct):
    width = conduct.shape[1]
    lane = lax.broadcasted_iota(jnp.int32, conduct.shape, 1)
    return 0.5 * (conduct + jnp.where(lane == width - 1, 0.0, pltpu.roll(conduct, width - 1, 1)))


def prepare_kernel(
    place_ref, perm_hbm, conc_hbm, wells_hbm, data_hbm, var_hbm, noise_hbm,
    near_ref, far_ref, near_edge_ref, far_edge_ref, low_ref, part_ref, conduct_ref, here_ref, wells_ref, data_ref, var_ref, noise_ref,
    perm_ref, conc_ref, sem,
):
    main = [
        pltpu.make_async_copy(source.at[row], target.at[row], sem.at[2 * i + row])
        for i, (source, target) in enumerate(((perm_hbm, perm_ref), (conc_hbm, conc_ref)))
        for row in range(2)
    ]
    small = [
        pltpu.make_async_copy(source, target, sem.at[4 + i])
        for i, (source, target) in enumerate(
            ((wells_hbm, wells_ref), (data_hbm, data_ref), (var_hbm, var_ref), (noise_hbm, noise_ref))
        )
    ]
    for copy in main + small:
        copy.start()
    for copy in main:
        copy.wait()
    perm0, perm1 = perm_ref[0], perm_ref[1]
    conc0, conc1 = conc_ref[0], conc_ref[1]
    low_ref[0], low_ref[1] = perm0.astype(BF16), perm1.astype(BF16)
    cond0, cond1 = jnp.exp(perm0), jnp.exp(perm1)
    conduct_ref[0], conduct_ref[1] = cond0, cond1
    between = 0.5 * (cond0 + cond1) * (conc1 - conc0)
    part0 = conc0 + time_step * (along_row(conc0, link_right(cond0), 0.5 * cond0) + between)
    part1 = conc1 + time_step * (along_row(conc1, link_right(cond1), 0.5 * cond1) - between)
    part_ref[0], part_ref[1] = part0, part1
    even = lax.rem(place_ref[0], 2) == 0
    edges = ((conc0, conc1), (cond0, cond1), (part0, part1))
    for i, (low_edge, high_edge) in enumerate(edges):
        near_edge_ref[i] = jnp.where(even, high_edge, low_edge).astype(BF16)
        far_edge_ref[i] = jnp.where(even, low_edge, high_edge).astype(BF16)
    for copy in small:
        copy.wait()
    members, width = conc0.shape
    pieces = []
    for pair in edges:
        for row in pair:
            high = row.astype(BF16)
            pieces += [high, (row - high.astype(F32)).astype(BF16)]
    pieces = jnp.concatenate(pieces, axis=0)
    column = lax.rem(wells_ref[...], width)
    chunk = 256
    total = [jnp.zeros((pieces.shape[0], 128), F32) for _ in range(3)]
    for start in range(0, width, chunk):
        position = lax.broadcasted_iota(jnp.int32, (chunk, 128), 0) + (start - column)
        for side in range(3):
            chosen = jnp.where(position == side - 1, 1.0, 0.0).astype(BF16)
            total[side] = total[side] + jnp.dot(
                pieces[:, start : start + chunk], chosen, preferred_element_type=F32
            )
    values = [
        [t[2 * members * q : 2 * members * q + members] + t[2 * members * q + members : 2 * members * (q + 1)] for q in range(6)]
        for t in total
    ]
    for side in range(3):
        for quantity in range(6):
            here_ref[6 * side + quantity] = values[side][quantity]
    for slot, (side, quantity) in enumerate(SENT):
        low_value, high_value = values[side][2 * quantity], values[side][2 * quantity + 1]
        near_ref[slot] = jnp.where(even, high_value, low_value).astype(BF16)
        far_ref[slot] = jnp.where(even, low_value, high_value).astype(BF16)


def combine_kernel(width, place_ref, near_ref, far_ref, here_ref, wells_ref, out_ref):
    strip = place_ref[0]
    even = lax.rem(strip, 2) == 0
    row = jnp.broadcast_to(wells_ref[...], here_ref.shape[1:]) // width
    upper = lax.rem(row, 2) == 0
    near = [near_ref[i].astype(F32) for i in range(len(SENT))]
    far = [far_ref[i].astype(F32) for i in range(len(SENT))]
    above = [jnp.where(even, f, n) for n, f in zip(near, far)]
    below = [jnp.where(even, n, f) for n, f in zip(near, far)]
    beside = [jnp.where(upper, a, b) for a, b in zip(above, below)]
    beyond = [jnp.where(upper, b, a) for a, b in zip(above, below)]
    conc_n, cond_n, part_n, conc_nl, cond_nl, conc_nr, cond_nr = beside
    conc_f, cond_f = beyond[0], beyond[1]

    def own(side, quantity):
        return jnp.where(upper, here_ref[6 * side + 2 * quantity], here_ref[6 * side + 2 * quantity + 1])

    def other(side, quantity):
        return jnp.where(upper, here_ref[6 * side + 2 * quantity + 1], here_ref[6 * side + 2 * quantity])

    half = 0.5 * time_step
    conc, cond, part = own(1, 0), own(1, 1), own(1, 2)
    conc_l, cond_l, part_l = own(0, 0), own(0, 1), own(0, 2)
    conc_r, cond_r, part_r = own(2, 0), own(2, 1), own(2, 2)
    conc_o, cond_o, part_o = other(1, 0), other(1, 1), other(1, 2)
    gain = half * (cond + cond_n) * (conc_n - conc)
    outside = (row == 0) | (row == 2 * STRIPS - 1)
    once = part + gain
    once_n = jnp.where(outside, 0.0, part_n - gain)
    once_l = part_l + half * (cond_l + cond_nl) * (conc_nl - conc_l)
    once_r = part_r + half * (cond_r + cond_nr) * (conc_nr - conc_r)
    once_o = part_o + half * (cond_o + cond_f) * (conc_f - conc_o)
    twice = once + half * (
        (cond + cond_n) * (once_n - once)
        + (cond + cond_o) * (once_o - once)
        + (cond + cond_l) * (once_l - once)
        + (cond + cond_r) * (once_r - once)
    )
    picked = jnp.where(row // 2 == strip, twice, 0.0)
    for copy in range(out_ref.shape[0]):
        out_ref[copy] = picked


def combine(place, near, far, here, wells, width, copies):
    return pl.pallas_call(
        functools.partial(combine_kernel, width),
        out_shape=jax.ShapeDtypeStruct((copies, *here.shape[1:]), F32),
        in_specs=[pl.BlockSpec(memory_space=pltpu.SMEM)] + [pl.BlockSpec(memory_space=pltpu.VMEM)] * 4,
        cost_estimate=pl.CostEstimate(flops=100_000, bytes_accessed=500_000, transcendentals=0),
        compiler_params=pltpu.CompilerParams(vmem_limit_bytes=VMEM_LIMIT),
        name="combine",
    )(place, near, far, here, wells)


def prepare(place, log_perm, conc, wells, obs_data, obs_var, noise):
    rows, members, width = log_perm.shape
    edge = jax.ShapeDtypeStruct((3, members, width), BF16)
    full = jax.ShapeDtypeStruct(log_perm.shape, F32)
    sent = jax.ShapeDtypeStruct((len(SENT), members, 128), BF16)
    here = jax.ShapeDtypeStruct((18, members, 128), F32)
    small = [jax.ShapeDtypeStruct(a.shape, a.dtype) for a in (wells, obs_data, obs_var, noise)]
    return pl.pallas_call(
        prepare_kernel,
        out_shape=(sent, sent, edge, edge, jax.ShapeDtypeStruct(log_perm.shape, BF16), full, full, here, *small),
        in_specs=[pl.BlockSpec(memory_space=pltpu.SMEM)] + [pl.BlockSpec(memory_space=pltpu.HBM)] * 6,
        out_specs=[pl.BlockSpec(memory_space=pltpu.VMEM)] * 12,
        scratch_shapes=[
            pltpu.VMEM(log_perm.shape, F32),
            pltpu.VMEM(log_perm.shape, F32),
            pltpu.SemaphoreType.DMA((8,)),
        ],
        cost_estimate=pl.CostEstimate(flops=2_000_000, bytes_accessed=1_600_000, transcendentals=65536),
        compiler_params=pltpu.CompilerParams(vmem_limit_bytes=VMEM_LIMIT),
        name="prepare",
    )(place, *[pltpu.with_memory_space_constraint(a, pltpu.HBM) for a in (log_perm, conc, wells, obs_data, obs_var, noise)])


def spread_kernel(found_ref, out_ref):
    total = found_ref[0]
    for i in range(1, found_ref.shape[0]):
        total = total + found_ref[i]
    for copy in range(out_ref.shape[0]):
        out_ref[copy] = total


def spread(found, copies):
    return pl.pallas_call(
        spread_kernel,
        out_shape=jax.ShapeDtypeStruct((copies, *found.shape[1:]), F32),
        cost_estimate=pl.CostEstimate(flops=65536, bytes_accessed=400_000, transcendentals=0),
        compiler_params=pltpu.CompilerParams(vmem_limit_bytes=VMEM_LIMIT),
        name="spread",
    )(found)


def advance_kernel(place_ref, conc_ref, conduct_ref, part_ref, near_ref, far_ref, out_ref):
    strip = place_ref[0]
    conc0, conc1 = conc_ref[0], conc_ref[1]
    cond0, cond1 = conduct_ref[0], conduct_ref[1]
    even = lax.rem(strip, 2) == 0
    near = [near_ref[i].astype(F32) for i in range(3)]
    far = [far_ref[i].astype(F32) for i in range(3)]
    conc_a, cond_a, part_a = [jnp.where(even, f, n) for n, f in zip(near, far)]
    conc_b, cond_b, part_b = [jnp.where(even, n, f) for n, f in zip(near, far)]
    link_a = 0.5 * (cond0 + cond_a)
    link_b = 0.5 * (cond1 + cond_b)
    gain_a = time_step * (link_a * (conc_a - conc0))
    gain_b = time_step * (link_b * (conc_b - conc1))
    once0, once1 = part_ref[0] + gain_a, part_ref[1] + gain_b
    once_a = jnp.where(strip == 0, 0.0, part_a - gain_a)
    once_b = jnp.where(strip == STRIPS - 1, 0.0, part_b - gain_b)
    between = 0.5 * (cond0 + cond1) * (once1 - once0)
    twice0 = once0 + time_step * (
        along_row(once0, link_right(cond0), 0.5 * cond0) + between + link_a * (once_a - once0)
    )
    twice1 = once1 + time_step * (
        along_row(once1, link_right(cond1), 0.5 * cond1) - between + link_b * (once_b - once1)
    )
    out_ref[0], out_ref[1] = twice0, twice1


def advance(place, conc, conduct, part, near, far):
    vmem = pl.BlockSpec(memory_space=pltpu.VMEM)
    return pl.pallas_call(
        advance_kernel,
        out_shape=jax.ShapeDtypeStruct(conc.shape, F32),
        in_specs=[pl.BlockSpec(memory_space=pltpu.SMEM)] + [vmem] * 5,
        out_specs=vmem,
        cost_estimate=pl.CostEstimate(flops=4_000_000, bytes_accessed=1_800_000, transcendentals=0),
        compiler_params=pltpu.CompilerParams(vmem_limit_bytes=VMEM_LIMIT),
        name="advance",
    )(place, conc, conduct, part, near, far)


def update_kernel(place_ref, found_ref, noise_ref, data_ref, var_ref, perm_ref, even_ref, odd_ref, out_ref, pred, work, solved, low, sem):
    group = place_ref[1]
    copies = []
    for position in range(8):
        source = (even_ref if position < 4 else odd_ref).at[position % 4]
        for row in range(2):
            copies.append(
                pltpu.make_async_copy(source.at[row], low.at[row, pl.ds(position * 16, 16)], sem.at[position, row])
            )
    for copy in copies:
        copy.start()
    for position in range(8):
        block = lax.bitwise_xor(group, 2 * position if position < 4 else 2 * position - 7)
        pred[pl.ds(position * 16, 16), :] = found_ref[2 * block] + found_ref[2 * block + 1]
    own = found_ref[2 * group] + found_ref[2 * group + 1]
    centred = weights_of(pred[...], own, noise_ref[...], data_ref[...], var_ref[...], work, solved).astype(BF16)
    for copy in copies:
        copy.wait()
    for row in range(2):
        out_ref[row] = perm_ref[row] + jnp.dot(centred, low[row], preferred_element_type=F32)


def update(place, found, noise, obs_data, obs_var, log_perm, even, odd):
    vmem = pl.BlockSpec(memory_space=pltpu.VMEM)
    anywhere = pl.BlockSpec(memory_space=pl.ANY)
    rows, members, width = log_perm.shape
    return pl.pallas_call(
        update_kernel,
        out_shape=jax.ShapeDtypeStruct(log_perm.shape, F32),
        in_specs=[pl.BlockSpec(memory_space=pltpu.SMEM)] + [vmem] * 5 + [anywhere] * 2,
        out_specs=vmem,
        scratch_shapes=[
            pltpu.VMEM((128, 128), F32),
            pltpu.VMEM((128, 384), F32),
            pltpu.VMEM((128, 256), F32),
            pltpu.VMEM((rows, 128, width), BF16),
            pltpu.SemaphoreType.DMA((8, 2)),
        ],
        cost_estimate=pl.CostEstimate(flops=200_000_000, bytes_accessed=1_700_000, transcendentals=128),
        compiler_params=pltpu.CompilerParams(vmem_limit_bytes=VMEM_LIMIT),
        name="update",
    )(place, found, noise, obs_data, obs_var, log_perm, even, odd)


STRIPS = 64


def swapped(value, axis, first, count):
    pairs = [(i, i + 1) for i in range(first, count - 1, 2)]
    return lax.ppermute(value, axis, pairs + [(high, low) for low, high in pairs])


def crossed(value, flip):
    return lax.ppermute(value, "z_lo", [(i, i ^ flip) for i in range(4)])


def local(log_perm, concentration, well_cells, obs_data, obs_var, obs_noise):
    place = jnp.stack([lax.axis_index(SPACE), lax.axis_index(MEM)]).astype(jnp.int32)
    near, far, near_edge, far_edge, low, part, conduct, here, wells, data, var, noise = prepare(
        place, log_perm, concentration, well_cells[None], obs_data[None], obs_var[None], obs_noise
    )
    far = swapped(far, SPACE, 1, STRIPS)
    near = swapped(near, SPACE, 0, STRIPS)
    picked = combine(place, near, far, here, wells, log_perm.shape[2], 32)
    near_edge, far_edge, picked = lax.optimization_barrier((near_edge, far_edge, picked))
    found = lax.all_to_all(picked, ("x", "y"), 0, 0, tiled=True)
    far_edge = swapped(far_edge, SPACE, 1, STRIPS)
    near_edge = swapped(near_edge, SPACE, 0, STRIPS)
    even = jnp.stack([low] + [crossed(low, flip) for flip in (1, 2, 3)])
    even, found = lax.optimization_barrier((even, found))
    found = lax.all_to_all(spread(found, 16), ("z_lo", "core", "z_hi"), 0, 0, tiled=True)
    odd = swapped(even, "core", 0, 2)
    updated = update(place, found, noise, data, var, log_perm, even, odd)
    near_edge, far_edge, updated = lax.optimization_barrier((near_edge, far_edge, updated))
    tracer = advance(place, concentration, conduct, part, near_edge, far_edge)
    return (tracer, updated)


def solution(mesh):
    fine = Mesh(mesh.devices.reshape(4, 2, 2, 4, 8), MEM + SPACE)
    return jax.shard_map(
        local,
        mesh=fine,
        in_specs=(P(SPACE, MEM, None), P(SPACE, MEM, None), P(), P(), P(), P(MEM, None)),
        out_specs=(P(SPACE, MEM, None), P(SPACE, MEM, None)),
        check_vma=False,
    )
```

```python
import jax
import jax.numpy as jnp
from jax import lax
from jax.experimental import pallas as pl
from jax.experimental.pallas import tpu as pltpu
from jax.sharding import Mesh, PartitionSpec as P

F32, BF16 = jnp.float32, jnp.bfloat16
time_step = 0.03
inflation = 4.0
HIGH = lax.Precision.HIGHEST
TN = (((0,), (0,)), ((), ()))
PANEL = 16
MEM = ("z_lo", "core")
SPACE = ("z_hi", "x", "y")
ORDER = (0, 2, 4, 6, 1, 3, 5, 7)
VMEM_LIMIT = 48 * 1024 * 1024

def split3(x):
    hi = x.astype(BF16)
    rest = x - hi.astype(F32)
    mid = rest.astype(BF16)
    low = (rest - mid.astype(F32)).astype(BF16)
    return hi, mid, low


def factor_panel(rows, base):
    height = rows.shape[0]
    index = lax.broadcasted_iota(jnp.int32, (height, 128), 0)
    lanes = rows.shape[1] // 128
    cols = [jnp.broadcast_to(rows[:, base + c : base + c + 1], (height, 128)) for c in range(height)]
    tiles = [rows[:, t * 128 : (t + 1) * 128] for t in range(lanes)]
    for k in range(height):
        scale = lax.rsqrt(cols[k][k : k + 1, :])
        below = cols[k] * scale
        masked = jnp.where(index > k, below, 0.0)
        for c in range(k + 1, height):
            cols[c] = cols[c] - masked * below[c : c + 1, :]
        for t in range(lanes):
            top = tiles[t][k : k + 1, :] * scale
            tiles[t] = jnp.where(index == k, top, tiles[t] - masked * top)
    return jnp.concatenate(tiles, axis=1)


def weights_of(pred, own, own_noise, obs_data, obs_var, work, solved):
    members = pred.shape[0]
    anomaly = pred - jnp.mean(pred, axis=0, keepdims=True)
    innovation = obs_data + jnp.sqrt(inflation * obs_var) * own_noise - own
    cov = lax.dot_general(anomaly, anomaly, TN, precision=HIGH, preferred_element_type=F32) / (members - 1)
    r = lax.broadcasted_iota(jnp.int32, (128, 128), 0)
    c = lax.broadcasted_iota(jnp.int32, (128, 128), 1)
    cov = cov + jnp.where(r == c, jnp.broadcast_to(inflation * obs_var, (128, 128)), 0.0)
    work[:, 0:128] = cov
    work[:, 128:256] = anomaly.T
    padded = jnp.concatenate([innovation, jnp.zeros((112, 128), F32)], axis=0)
    work[:, 256:384] = padded.T
    for p in range(128 // PANEL):
        u = factor_panel(work[p * PANEL : (p + 1) * PANEL, :], p * PANEL)
        solved[p * PANEL : (p + 1) * PANEL, :] = u[:, 128:384]
        if p < 128 // PANEL - 1:
            h, m, l = split3(u)
            left = jnp.concatenate([h, h, m, h, l, m], axis=0)[:, 0:128]
            right = jnp.concatenate([h, m, h, l, h, m], axis=0)
            update = lax.dot_general(left, right, TN, preferred_element_type=F32)
            work[(p + 1) * PANEL :, :] = work[(p + 1) * PANEL :, :] - update[(p + 1) * PANEL :, :]
    w = lax.dot_general(
        solved[:, 128:256], solved[:, 0:128], TN, precision=HIGH, preferred_element_type=F32
    )[:16] / (members - 1)
    return w - jnp.mean(w, axis=1, keepdims=True)


def along_row(conc, link, left_edge):
    width = conc.shape[1]
    lane = lax.broadcasted_iota(jnp.int32, conc.shape, 1)
    right = jnp.where(lane == width - 1, 0.0, pltpu.roll(conc, width - 1, 1))
    flux = link * (right - conc)
    from_left = jnp.where(lane == 0, left_edge * conc, pltpu.roll(flux, 1, 1))
    return flux - from_left


def link_right(conduct):
    width = conduct.shape[1]
    lane = lax.broadcasted_iota(jnp.int32, conduct.shape, 1)
    return 0.5 * (conduct + jnp.where(lane == width - 1, 0.0, pltpu.roll(conduct, width - 1, 1)))


def prepare_kernel(
    place_ref, perm_hbm, conc_hbm, wells_hbm, data_hbm, var_hbm, noise_hbm,
    near_ref, far_ref, low_ref, part_ref, conduct_ref, wells_ref, data_ref, var_ref, noise_ref,
    perm_ref, conc_ref, sem,
):
    main = [
        pltpu.make_async_copy(source.at[row], target.at[row], sem.at[2 * i + row])
        for i, (source, target) in enumerate(((perm_hbm, perm_ref), (conc_hbm, conc_ref)))
        for row in range(2)
    ]
    small = [
        pltpu.make_async_copy(source, target, sem.at[4 + i])
        for i, (source, target) in enumerate(
            ((wells_hbm, wells_ref), (data_hbm, data_ref), (var_hbm, var_ref), (noise_hbm, noise_ref))
        )
    ]
    for copy in main + small:
        copy.start()
    for copy in main:
        copy.wait()
    perm0, perm1 = perm_ref[0], perm_ref[1]
    conc0, conc1 = conc_ref[0], conc_ref[1]
    low_ref[0], low_ref[1] = perm0.astype(BF16), perm1.astype(BF16)
    cond0, cond1 = jnp.exp(perm0), jnp.exp(perm1)
    conduct_ref[0], conduct_ref[1] = cond0, cond1
    between = 0.5 * (cond0 + cond1) * (conc1 - conc0)
    part0 = conc0 + time_step * (along_row(conc0, link_right(cond0), 0.5 * cond0) + between)
    part1 = conc1 + time_step * (along_row(conc1, link_right(cond1), 0.5 * cond1) - between)
    part_ref[0], part_ref[1] = part0, part1
    even = lax.rem(place_ref[0], 2) == 0
    for i, (low_edge, high_edge) in enumerate(((conc0, conc1), (cond0, cond1), (part0, part1))):
        near_ref[i] = jnp.where(even, high_edge, low_edge).astype(BF16)
        far_ref[i] = jnp.where(even, low_edge, high_edge).astype(BF16)
    for copy in small:
        copy.wait()


def prepare(place, log_perm, conc, wells, obs_data, obs_var, noise):
    rows, members, width = log_perm.shape
    edge = jax.ShapeDtypeStruct((3, members, width), BF16)
    full = jax.ShapeDtypeStruct(log_perm.shape, F32)
    small = [jax.ShapeDtypeStruct(a.shape, a.dtype) for a in (wells, obs_data, obs_var, noise)]
    return pl.pallas_call(
        prepare_kernel,
        out_shape=(edge, edge, jax.ShapeDtypeStruct(log_perm.shape, BF16), full, full, *small),
        in_specs=[pl.BlockSpec(memory_space=pltpu.SMEM)] + [pl.BlockSpec(memory_space=pltpu.HBM)] * 6,
        out_specs=[pl.BlockSpec(memory_space=pltpu.VMEM)] * 9,
        scratch_shapes=[
            pltpu.VMEM(log_perm.shape, F32),
            pltpu.VMEM(log_perm.shape, F32),
            pltpu.SemaphoreType.DMA((8,)),
        ],
        cost_estimate=pl.CostEstimate(flops=2_000_000, bytes_accessed=1_600_000, transcendentals=65536),
        compiler_params=pltpu.CompilerParams(vmem_limit_bytes=VMEM_LIMIT),
        name="prepare",
    )(place, *[pltpu.with_memory_space_constraint(a, pltpu.HBM) for a in (log_perm, conc, wells, obs_data, obs_var, noise)])


def spread_kernel(found_ref, out_ref):
    total = found_ref[0]
    for i in range(1, found_ref.shape[0]):
        total = total + found_ref[i]
    for copy in range(out_ref.shape[0]):
        out_ref[copy] = total


def spread(found, copies):
    return pl.pallas_call(
        spread_kernel,
        out_shape=jax.ShapeDtypeStruct((copies, *found.shape[1:]), F32),
        cost_estimate=pl.CostEstimate(flops=65536, bytes_accessed=400_000, transcendentals=0),
        compiler_params=pltpu.CompilerParams(vmem_limit_bytes=VMEM_LIMIT),
        name="spread",
    )(found)


def advance_kernel(place_ref, conc_ref, conduct_ref, part_ref, far_ref, near_ref, wells_ref, out_ref, picked_ref):
    strip = place_ref[0]
    conc0, conc1 = conc_ref[0], conc_ref[1]
    cond0, cond1 = conduct_ref[0], conduct_ref[1]
    even = lax.rem(strip, 2) == 0
    near = [near_ref[i].astype(F32) for i in range(3)]
    far = [far_ref[i].astype(F32) for i in range(3)]
    conc_a, cond_a, part_a = [jnp.where(even, f, n) for n, f in zip(near, far)]
    conc_b, cond_b, part_b = [jnp.where(even, n, f) for n, f in zip(near, far)]
    link_a = 0.5 * (cond0 + cond_a)
    link_b = 0.5 * (cond1 + cond_b)
    gain_a = time_step * (link_a * (conc_a - conc0))
    gain_b = time_step * (link_b * (conc_b - conc1))
    once0, once1 = part_ref[0] + gain_a, part_ref[1] + gain_b
    once_a = jnp.where(strip == 0, 0.0, part_a - gain_a)
    once_b = jnp.where(strip == STRIPS - 1, 0.0, part_b - gain_b)
    between = 0.5 * (cond0 + cond1) * (once1 - once0)
    twice0 = once0 + time_step * (
        along_row(once0, link_right(cond0), 0.5 * cond0) + between + link_a * (once_a - once0)
    )
    twice1 = once1 + time_step * (
        along_row(once1, link_right(cond1), 0.5 * cond1) - between + link_b * (once_b - once1)
    )
    out_ref[0], out_ref[1] = twice0, twice1
    members, width = twice0.shape
    chunk = 256
    total = jnp.zeros((3 * members, 128), F32)
    for row, values in enumerate((twice0, twice1)):
        pieces = jnp.concatenate(split3(values), axis=0)
        column = wells_ref[...] - (2 * strip + row) * width
        for start in range(0, width, chunk):
            here = lax.broadcasted_iota(jnp.int32, (chunk, 128), 0) + start
            chosen = jnp.where(here == column, 1.0, 0.0).astype(BF16)
            total = total + jnp.dot(pieces[:, start : start + chunk], chosen, preferred_element_type=F32)
    picked = total[:members] + total[members : 2 * members] + total[2 * members :]
    for copy in range(picked_ref.shape[0]):
        picked_ref[copy] = picked


def advance(place, conc, conduct, part, far, near, wells, copies):
    vmem = pl.BlockSpec(memory_space=pltpu.VMEM)
    return pl.pallas_call(
        advance_kernel,
        out_shape=(
            jax.ShapeDtypeStruct(conc.shape, F32),
            jax.ShapeDtypeStruct((copies, conc.shape[1], 128), F32),
        ),
        in_specs=[pl.BlockSpec(memory_space=pltpu.SMEM)] + [vmem] * 6,
        out_specs=(vmem, vmem),
        cost_estimate=pl.CostEstimate(flops=60_000_000, bytes_accessed=1_800_000, transcendentals=0),
        compiler_params=pltpu.CompilerParams(vmem_limit_bytes=VMEM_LIMIT),
        name="advance",
    )(place, conc, conduct, part, far, near, wells)


def solve_kernel(place_ref, found_ref, noise_ref, data_ref, var_ref, out_ref, pred, work, solved):
    group = place_ref[1]
    for position, flip in enumerate(ORDER):
        block = lax.bitwise_xor(group, flip)
        pred[pl.ds(position * 16, 16), :] = found_ref[2 * block] + found_ref[2 * block + 1]
    centred = weights_of(pred[...], pred[0:16], noise_ref[...], data_ref[...], var_ref[...], work, solved)
    out_ref[...] = centred.astype(BF16)


def solve(place, found, noise, obs_data, obs_var):
    vmem = pl.BlockSpec(memory_space=pltpu.VMEM)
    return pl.pallas_call(
        solve_kernel,
        out_shape=jax.ShapeDtypeStruct((16, 128), BF16),
        in_specs=[pl.BlockSpec(memory_space=pltpu.SMEM)] + [vmem] * 4,
        out_specs=vmem,
        scratch_shapes=[
            pltpu.VMEM((128, 128), F32),
            pltpu.VMEM((128, 384), F32),
            pltpu.VMEM((128, 256), F32),
        ],
        cost_estimate=pl.CostEstimate(flops=50_000_000, bytes_accessed=18_000_000, transcendentals=128),
        compiler_params=pltpu.CompilerParams(vmem_limit_bytes=VMEM_LIMIT),
        name="solve",
    )(place, found, noise, obs_data, obs_var)


def increment_kernel(weights_ref, perm_ref, *refs):
    *pieces, odd_ref, out_ref = refs
    for row in range(2):
        members = [piece[row] for piece in pieces] + [odd_ref[i, row] for i in range(odd_ref.shape[0])]
        stacked = jnp.concatenate(members, axis=0)
        out_ref[row] = perm_ref[row] + jnp.dot(weights_ref[...], stacked, preferred_element_type=F32)


def increment(weights, log_perm, pieces, odd):
    return pl.pallas_call(
        increment_kernel,
        out_shape=jax.ShapeDtypeStruct(log_perm.shape, F32),
        cost_estimate=pl.CostEstimate(flops=20_000_000, bytes_accessed=1_700_000, transcendentals=0),
        compiler_params=pltpu.CompilerParams(vmem_limit_bytes=VMEM_LIMIT),
        name="increment",
    )(weights, log_perm, *pieces, odd)


STRIPS = 64


def swapped(value, axis, first, count):
    pairs = [(i, i + 1) for i in range(first, count - 1, 2)]
    return lax.ppermute(value, axis, pairs + [(high, low) for low, high in pairs])


def crossed(value, flip):
    return lax.ppermute(value, "z_lo", [(i, i ^ flip) for i in range(4)])


def local(log_perm, concentration, well_cells, obs_data, obs_var, obs_noise):
    place = jnp.stack([lax.axis_index(SPACE), lax.axis_index(MEM)]).astype(jnp.int32)
    near, far, low, part, conduct, wells, data, var, noise = prepare(
        place, log_perm, concentration, well_cells[None], obs_data[None], obs_var[None], obs_noise
    )
    far = swapped(far, SPACE, 1, STRIPS)
    near = swapped(near, SPACE, 0, STRIPS)
    tracer, picked = advance(place, concentration, conduct, part, far, near, wells, 32)
    found = lax.all_to_all(picked, ("x", "y"), 0, 0, tiled=True)
    even = [low] + [crossed(low, flip) for flip in (1, 2, 3)]
    found = lax.all_to_all(spread(found, 16), ("z_lo", "core", "z_hi"), 0, 0, tiled=True)
    odd = swapped(jnp.stack(even), "core", 0, 2)
    weights = solve(place, found, noise, data, var)
    updated = increment(weights, log_perm, even, odd)
    return (tracer, updated)


def solution(mesh):
    fine = Mesh(mesh.devices.reshape(4, 2, 2, 4, 8), MEM + SPACE)
    return jax.shard_map(
        local,
        mesh=fine,
        in_specs=(P(SPACE, MEM, None), P(SPACE, MEM, None), P(), P(), P(), P(MEM, None)),
        out_specs=(P(SPACE, MEM, None), P(SPACE, MEM, None)),
        check_vma=False,
    )
```

```python
import jax
import jax.numpy as jnp
from jax import lax
from jax.experimental import pallas as pl
from jax.experimental.pallas import tpu as pltpu
from jax.sharding import Mesh, PartitionSpec as P

F32, BF16 = jnp.float32, jnp.bfloat16
time_step = 0.03
inflation = 4.0
HIGH = lax.Precision.HIGHEST
TN = (((0,), (0,)), ((), ()))
PANEL = 16
GRAIN = 32000 / 6
MEM = ("z_lo", "core")
SPACE = ("z_hi", "x", "y")
ORDER = (0, 4, 6, 2, 1, 5, 7, 3)
VMEM_LIMIT = 48 * 1024 * 1024

def split3(x):
    hi = x.astype(BF16)
    rest = x - hi.astype(F32)
    mid = rest.astype(BF16)
    low = (rest - mid.astype(F32)).astype(BF16)
    return hi, mid, low


def factor_panel(rows, base):
    height = rows.shape[0]
    index = lax.broadcasted_iota(jnp.int32, (height, 128), 0)
    lanes = rows.shape[1] // 128
    cols = [jnp.broadcast_to(rows[:, base + c : base + c + 1], (height, 128)) for c in range(height)]
    tiles = [rows[:, t * 128 : (t + 1) * 128] for t in range(lanes)]
    for k in range(height):
        scale = lax.rsqrt(cols[k][k : k + 1, :])
        below = cols[k] * scale
        masked = jnp.where(index > k, below, 0.0)
        for c in range(k + 1, height):
            cols[c] = cols[c] - masked * below[c : c + 1, :]
        for t in range(lanes):
            top = tiles[t][k : k + 1, :] * scale
            tiles[t] = jnp.where(index == k, top, tiles[t] - masked * top)
    return jnp.concatenate(tiles, axis=1)


def weights_of(pred, own, own_noise, obs_data, obs_var, work, solved):
    members = pred.shape[0]
    anomaly = pred - jnp.mean(pred, axis=0, keepdims=True)
    innovation = obs_data + jnp.sqrt(inflation * obs_var) * own_noise - own
    cov = lax.dot_general(anomaly, anomaly, TN, precision=HIGH, preferred_element_type=F32) / (members - 1)
    r = lax.broadcasted_iota(jnp.int32, (128, 128), 0)
    c = lax.broadcasted_iota(jnp.int32, (128, 128), 1)
    cov = cov + jnp.where(r == c, jnp.broadcast_to(inflation * obs_var, (128, 128)), 0.0)
    work[:, 0:128] = cov
    work[:, 128:256] = anomaly.T
    padded = jnp.concatenate([innovation, jnp.zeros((112, 128), F32)], axis=0)
    work[:, 256:384] = padded.T
    for p in range(128 // PANEL):
        u = factor_panel(work[p * PANEL : (p + 1) * PANEL, :], p * PANEL)
        solved[p * PANEL : (p + 1) * PANEL, :] = u[:, 128:384]
        if p < 128 // PANEL - 1:
            h, m, l = split3(u)
            left = jnp.concatenate([h, h, m, h, l, m], axis=0)[:, 0:128]
            right = jnp.concatenate([h, m, h, l, h, m], axis=0)
            update = lax.dot_general(left, right, TN, preferred_element_type=F32)
            work[(p + 1) * PANEL :, :] = work[(p + 1) * PANEL :, :] - update[(p + 1) * PANEL :, :]
    w = lax.dot_general(
        solved[:, 128:256], solved[:, 0:128], TN, precision=HIGH, preferred_element_type=F32
    )[:16] / (members - 1)
    return w - jnp.mean(w, axis=1, keepdims=True)


def along_row(conc, link, left_edge):
    width = conc.shape[1]
    lane = lax.broadcasted_iota(jnp.int32, conc.shape, 1)
    right = jnp.where(lane == width - 1, 0.0, pltpu.roll(conc, width - 1, 1))
    flux = link * (right - conc)
    from_left = jnp.where(lane == 0, left_edge * conc, pltpu.roll(flux, 1, 1))
    return flux - from_left


def link_right(conduct):
    width = conduct.shape[1]
    lane = lax.broadcasted_iota(jnp.int32, conduct.shape, 1)
    return 0.5 * (conduct + jnp.where(lane == width - 1, 0.0, pltpu.roll(conduct, width - 1, 1)))


def prepare_kernel(
    perm_hbm, conc_hbm, wells_hbm, data_hbm, var_hbm, noise_hbm,
    near_ref, far_ref, low_ref, part_ref, conduct_ref, wells_ref, data_ref, var_ref, noise_ref,
    perm_ref, conc_ref, sem,
):
    main = [
        pltpu.make_async_copy(source.at[row], target.at[row], sem.at[2 * i + row])
        for i, (source, target) in enumerate(((perm_hbm, perm_ref), (conc_hbm, conc_ref)))
        for row in range(2)
    ]
    small = [
        pltpu.make_async_copy(source, target, sem.at[4 + i])
        for i, (source, target) in enumerate(
            ((wells_hbm, wells_ref), (data_hbm, data_ref), (var_hbm, var_ref), (noise_hbm, noise_ref))
        )
    ]
    for copy in main + small:
        copy.start()
    for copy in main:
        copy.wait()
    perm0, perm1 = perm_ref[0], perm_ref[1]
    conc0, conc1 = conc_ref[0], conc_ref[1]
    low_ref[0], low_ref[1] = perm0.astype(BF16), perm1.astype(BF16)
    cond0, cond1 = jnp.exp(perm0), jnp.exp(perm1)
    conduct_ref[0], conduct_ref[1] = cond0, cond1
    between = 0.5 * (cond0 + cond1) * (conc1 - conc0)
    part0 = conc0 + time_step * (along_row(conc0, link_right(cond0), 0.5 * cond0) + between)
    part1 = conc1 + time_step * (along_row(conc1, link_right(cond1), 0.5 * cond1) - between)
    part_ref[0], part_ref[1] = part0, part1
    even = lax.rem(lax.axis_index(SPACE), 2) == 0
    for i, (low_edge, high_edge) in enumerate(((conc0, conc1), (cond0, cond1), (part0, part1))):
        near_ref[i] = jnp.where(even, high_edge, low_edge).astype(BF16)
        far_ref[i] = jnp.where(even, low_edge, high_edge).astype(BF16)
    for copy in small:
        copy.wait()


def prepare(log_perm, conc, wells, obs_data, obs_var, noise):
    rows, members, width = log_perm.shape
    edge = jax.ShapeDtypeStruct((3, members, width), BF16)
    full = jax.ShapeDtypeStruct(log_perm.shape, F32)
    small = [jax.ShapeDtypeStruct(a.shape, a.dtype) for a in (wells, obs_data, obs_var, noise)]
    return pl.pallas_call(
        prepare_kernel,
        out_shape=(edge, edge, jax.ShapeDtypeStruct(log_perm.shape, BF16), full, full, *small),
        in_specs=[pl.BlockSpec(memory_space=pltpu.HBM)] * 6,
        out_specs=[pl.BlockSpec(memory_space=pltpu.VMEM)] * 9,
        scratch_shapes=[
            pltpu.VMEM(log_perm.shape, F32),
            pltpu.VMEM(log_perm.shape, F32),
            pltpu.SemaphoreType.DMA((8,)),
        ],
        cost_estimate=pl.CostEstimate(flops=2_000_000, bytes_accessed=1_600_000, transcendentals=65536),
        compiler_params=pltpu.CompilerParams(vmem_limit_bytes=VMEM_LIMIT),
        name="prepare",
    )(*[pltpu.with_memory_space_constraint(a, pltpu.HBM) for a in (log_perm, conc, wells, obs_data, obs_var, noise)])


def spread_kernel(found_ref, out_ref):
    total = found_ref[0]
    for i in range(1, found_ref.shape[0]):
        total = total + found_ref[i]
    for copy in range(out_ref.shape[0]):
        out_ref[copy] = total


def spread(found, copies):
    return pl.pallas_call(
        spread_kernel,
        out_shape=jax.ShapeDtypeStruct((copies, *found.shape[1:]), found.dtype),
        cost_estimate=pl.CostEstimate(flops=65536, bytes_accessed=400_000, transcendentals=0),
        compiler_params=pltpu.CompilerParams(vmem_limit_bytes=VMEM_LIMIT),
        name="spread",
    )(found)


def advance_kernel(conc_ref, conduct_ref, part_ref, far_ref, near_ref, wells_ref, out_ref, picked_ref):
    strip = lax.axis_index(SPACE)
    conc0, conc1 = conc_ref[0], conc_ref[1]
    cond0, cond1 = conduct_ref[0], conduct_ref[1]
    even = lax.rem(strip, 2) == 0
    near = [near_ref[i].astype(F32) for i in range(3)]
    far = [far_ref[i].astype(F32) for i in range(3)]
    conc_a, cond_a, part_a = [jnp.where(even, f, n) for n, f in zip(near, far)]
    conc_b, cond_b, part_b = [jnp.where(even, n, f) for n, f in zip(near, far)]
    link_a = 0.5 * (cond0 + cond_a)
    link_b = 0.5 * (cond1 + cond_b)
    gain_a = time_step * (link_a * (conc_a - conc0))
    gain_b = time_step * (link_b * (conc_b - conc1))
    once0, once1 = part_ref[0] + gain_a, part_ref[1] + gain_b
    once_a = jnp.where(strip == 0, 0.0, part_a - gain_a)
    once_b = jnp.where(strip == STRIPS - 1, 0.0, part_b - gain_b)
    between = 0.5 * (cond0 + cond1) * (once1 - once0)
    twice0 = once0 + time_step * (
        along_row(once0, link_right(cond0), 0.5 * cond0) + between + link_a * (once_a - once0)
    )
    twice1 = once1 + time_step * (
        along_row(once1, link_right(cond1), 0.5 * cond1) - between + link_b * (once_b - once1)
    )
    out_ref[0], out_ref[1] = twice0, twice1
    members, width = twice0.shape
    chunk = 256
    pieces = jnp.concatenate([*split3(twice0), *split3(twice1)], axis=0)
    cell = wells_ref[...] - 2 * strip * width
    column = jnp.where(cell >= width, cell - width, cell)
    total = jnp.zeros((6 * members, 128), F32)
    for start in range(0, width, chunk):
        here = lax.broadcasted_iota(jnp.int32, (chunk, 128), 0) + start
        chosen = jnp.where(here == column, 1.0, 0.0).astype(BF16)
        total = total + jnp.dot(pieces[:, start : start + chunk], chosen, preferred_element_type=F32)
    upper, lower = [
        total[i : i + members] + total[i + members : i + 2 * members] + total[i + 2 * members : i + 3 * members]
        for i in (0, 3 * members)
    ]
    picked = jnp.where(jnp.broadcast_to(cell, upper.shape) >= width, lower, upper)
    picked = jnp.round(picked * GRAIN).astype(jnp.int32).astype(jnp.int16)
    for copy in range(picked_ref.shape[0]):
        picked_ref[copy] = picked


def advance(conc, conduct, part, far, near, wells, copies):
    vmem = pl.BlockSpec(memory_space=pltpu.VMEM)
    return pl.pallas_call(
        advance_kernel,
        out_shape=(
            jax.ShapeDtypeStruct(conc.shape, F32),
            jax.ShapeDtypeStruct((copies, conc.shape[1], 128), jnp.int16),
        ),
        in_specs=[vmem] * 6,
        out_specs=(vmem, vmem),
        cost_estimate=pl.CostEstimate(flops=60_000_000, bytes_accessed=1_800_000, transcendentals=0),
        compiler_params=pltpu.CompilerParams(vmem_limit_bytes=VMEM_LIMIT),
        name="advance",
    )(conc, conduct, part, far, near, wells)


def solve_kernel(found_ref, noise_ref, data_ref, var_ref, out_ref, pred, work, solved):
    group = lax.axis_index(MEM)
    for position, flip in enumerate(ORDER):
        block = lax.bitwise_xor(group, flip)
        code = found_ref[2 * block].astype(jnp.int32) + found_ref[2 * block + 1].astype(jnp.int32)
        pred[pl.ds(position * 16, 16), :] = code.astype(F32) * (1 / GRAIN)
    centred = weights_of(pred[...], pred[0:16], noise_ref[...], data_ref[...], var_ref[...], work, solved)
    out_ref[...] = centred.astype(BF16)


def solve(found, noise, obs_data, obs_var):
    vmem = pl.BlockSpec(memory_space=pltpu.VMEM)
    return pl.pallas_call(
        solve_kernel,
        out_shape=jax.ShapeDtypeStruct((16, 128), BF16),
        in_specs=[vmem] * 4,
        out_specs=vmem,
        scratch_shapes=[
            pltpu.VMEM((128, 128), F32),
            pltpu.VMEM((128, 384), F32),
            pltpu.VMEM((128, 256), F32),
        ],
        cost_estimate=pl.CostEstimate(flops=50_000_000, bytes_accessed=18_000_000, transcendentals=128),
        compiler_params=pltpu.CompilerParams(vmem_limit_bytes=VMEM_LIMIT),
        name="solve",
    )(found, noise, obs_data, obs_var)


def increment_kernel(weights_ref, perm_ref, *refs):
    *pieces, out_ref = refs
    for row in range(2):
        members = [piece[i, row] for piece in pieces for i in range(piece.shape[0])]
        stacked = jnp.concatenate(members, axis=0)
        out_ref[row] = perm_ref[row] + jnp.dot(weights_ref[...], stacked, preferred_element_type=F32)


def increment(weights, log_perm, pieces):
    return pl.pallas_call(
        increment_kernel,
        out_shape=jax.ShapeDtypeStruct(log_perm.shape, F32),
        cost_estimate=pl.CostEstimate(flops=20_000_000, bytes_accessed=1_700_000, transcendentals=0),
        compiler_params=pltpu.CompilerParams(vmem_limit_bytes=VMEM_LIMIT),
        name="increment",
    )(weights, log_perm, *pieces)


STRIPS = 64
PLANES = [list(range(STRIPS // 2 - 1, -1, -1)), list(range(STRIPS // 2, STRIPS))]


def swapped(value, axis, first, count):
    pairs = [(i, i + 1) for i in range(first, count - 1, 2)]
    return lax.ppermute(value, axis, pairs + [(high, low) for low, high in pairs])


def crossed(value, flip):
    return lax.ppermute(value, "z_lo", [(i, i ^ flip) for i in range(4)])


def local(log_perm, concentration, well_cells, obs_data, obs_var, obs_noise):
    near, far, low, part, conduct, wells, data, var, noise = prepare(
        log_perm, concentration, well_cells[None], obs_data[None], obs_var[None], obs_noise
    )
    far = swapped(far, SPACE, 1, STRIPS)
    near = swapped(near, SPACE, 0, STRIPS)
    tracer, picked = advance(concentration, conduct, part, far, near, wells, 32)
    last, *pair = [crossed(low, flip) for flip in (1, 2, 3)]
    pair = jnp.stack(pair)
    found = lax.all_to_all(picked, SPACE, 0, 0, axis_index_groups=PLANES, tiled=True)
    found = lax.all_to_all(spread(found, 16), ("z_lo", "core", "z_hi"), 0, 0, tiled=True)
    mine = [low[None], pair, last[None]]
    pieces = mine + [swapped(piece, "core", 0, 2) for piece in mine]
    weights = solve(found, noise, data, var)
    updated = increment(weights, log_perm, pieces)
    return (tracer, updated)


def solution(mesh):
    fine = Mesh(mesh.devices.reshape(4, 2, 2, 4, 8), MEM + SPACE)
    return jax.shard_map(
        local,
        mesh=fine,
        in_specs=(P(SPACE, MEM, None), P(SPACE, MEM, None), P(), P(), P(), P(MEM, None)),
        out_specs=(P(SPACE, MEM, None), P(SPACE, MEM, None)),
        check_vma=False,
    )
```

```python
import jax
import jax.numpy as jnp
from jax import lax
from jax.experimental import pallas as pl
from jax.experimental.pallas import tpu as pltpu
from jax.sharding import Mesh, PartitionSpec as P

F32, BF16 = jnp.float32, jnp.bfloat16
time_step = 0.03
inflation = 4.0
HIGH = lax.Precision.HIGHEST
TN = (((0,), (0,)), ((), ()))
PANEL = 32
GRAIN = 32000 / 6
MEM = ("z_lo", "core")
SPACE = ("z_hi", "x", "y")
ORDER = (0, 4, 6, 2, 1, 5, 7, 3)
VMEM_LIMIT = 48 * 1024 * 1024

def split3(x):
    hi = x.astype(BF16)
    rest = x - hi.astype(F32)
    mid = rest.astype(BF16)
    low = (rest - mid.astype(F32)).astype(BF16)
    return hi, mid, low


def factor_panel(rows, base):
    height = rows.shape[0]
    index = lax.broadcasted_iota(jnp.int32, (height, 128), 0)
    lanes = rows.shape[1] // 128
    cols = [jnp.broadcast_to(rows[:, base + c : base + c + 1], (height, 128)) for c in range(height)]
    tiles = [rows[:, t * 128 : (t + 1) * 128] for t in range(lanes)]
    for k in range(height):
        scale = lax.rsqrt(cols[k][k : k + 1, :])
        below = cols[k] * scale
        masked = jnp.where(index > k, below, 0.0)
        for c in range(k + 1, height):
            cols[c] = cols[c] - masked * below[c : c + 1, :]
        for t in range(lanes):
            top = tiles[t][k : k + 1, :] * scale
            tiles[t] = jnp.where(index == k, top, tiles[t] - masked * top)
    return jnp.concatenate(tiles, axis=1)


def weights_of(pred, own, own_noise, obs_data, obs_var, work, solved):
    members = pred.shape[0]
    anomaly = pred - jnp.mean(pred, axis=0, keepdims=True)
    innovation = obs_data + jnp.sqrt(inflation * obs_var) * own_noise - own
    cov = lax.dot_general(anomaly, anomaly, TN, precision=HIGH, preferred_element_type=F32) / (members - 1)
    r = lax.broadcasted_iota(jnp.int32, (128, 128), 0)
    c = lax.broadcasted_iota(jnp.int32, (128, 128), 1)
    cov = cov + jnp.where(r == c, jnp.broadcast_to(inflation * obs_var, (128, 128)), 0.0)
    work[:, 0:128] = cov
    work[:, 128:256] = anomaly.T
    padded = jnp.concatenate([innovation, jnp.zeros((112, 128), F32)], axis=0)
    work[:, 256:384] = padded.T
    for p in range(128 // PANEL):
        u = factor_panel(work[p * PANEL : (p + 1) * PANEL, :], p * PANEL)
        solved[p * PANEL : (p + 1) * PANEL, :] = u[:, 128:384]
        if p < 128 // PANEL - 1:
            h, m, l = split3(u)
            left = jnp.concatenate([h, h, m, h, l, m], axis=0)[:, 0:128]
            right = jnp.concatenate([h, m, h, l, h, m], axis=0)
            update = lax.dot_general(left, right, TN, preferred_element_type=F32)
            work[(p + 1) * PANEL :, :] = work[(p + 1) * PANEL :, :] - update[(p + 1) * PANEL :, :]
    w = lax.dot_general(
        solved[:, 128:256], solved[:, 0:128], TN, precision=HIGH, preferred_element_type=F32
    )[:16] / (members - 1)
    return w - jnp.mean(w, axis=1, keepdims=True)


def along_row(conc, link, left_edge):
    width = conc.shape[1]
    lane = lax.broadcasted_iota(jnp.int32, conc.shape, 1)
    right = jnp.where(lane == width - 1, 0.0, pltpu.roll(conc, width - 1, 1))
    flux = link * (right - conc)
    from_left = jnp.where(lane == 0, left_edge * conc, pltpu.roll(flux, 1, 1))
    return flux - from_left


def link_right(conduct):
    width = conduct.shape[1]
    lane = lax.broadcasted_iota(jnp.int32, conduct.shape, 1)
    return 0.5 * (conduct + jnp.where(lane == width - 1, 0.0, pltpu.roll(conduct, width - 1, 1)))


def prepare_kernel(
    perm_hbm, conc_hbm, wells_hbm, data_hbm, var_hbm, noise_hbm,
    near_ref, far_ref, low_ref, part_ref, conduct_ref, wells_ref, data_ref, var_ref, noise_ref,
    perm_ref, conc_ref, sem,
):
    main = [
        pltpu.make_async_copy(source.at[row], target.at[row], sem.at[2 * i + row])
        for i, (source, target) in enumerate(((perm_hbm, perm_ref), (conc_hbm, conc_ref)))
        for row in range(2)
    ]
    small = [
        pltpu.make_async_copy(source, target, sem.at[4 + i])
        for i, (source, target) in enumerate(
            ((wells_hbm, wells_ref), (data_hbm, data_ref), (var_hbm, var_ref), (noise_hbm, noise_ref))
        )
    ]
    for copy in main + small:
        copy.start()
    for copy in main:
        copy.wait()
    perm0, perm1 = perm_ref[0], perm_ref[1]
    conc0, conc1 = conc_ref[0], conc_ref[1]
    low_ref[0], low_ref[1] = perm0.astype(BF16), perm1.astype(BF16)
    cond0, cond1 = jnp.exp(perm0), jnp.exp(perm1)
    conduct_ref[0], conduct_ref[1] = cond0, cond1
    between = 0.5 * (cond0 + cond1) * (conc1 - conc0)
    part0 = conc0 + time_step * (along_row(conc0, link_right(cond0), 0.5 * cond0) + between)
    part1 = conc1 + time_step * (along_row(conc1, link_right(cond1), 0.5 * cond1) - between)
    part_ref[0], part_ref[1] = part0, part1
    even = lax.rem(lax.axis_index(SPACE), 2) == 0
    for i, (low_edge, high_edge) in enumerate(((conc0, conc1), (cond0, cond1), (part0, part1))):
        near_ref[i] = jnp.where(even, high_edge, low_edge).astype(BF16)
        far_ref[i] = jnp.where(even, low_edge, high_edge).astype(BF16)
    for copy in small:
        copy.wait()


def prepare(log_perm, conc, wells, obs_data, obs_var, noise):
    rows, members, width = log_perm.shape
    edge = jax.ShapeDtypeStruct((3, members, width), BF16)
    full = jax.ShapeDtypeStruct(log_perm.shape, F32)
    small = [jax.ShapeDtypeStruct(a.shape, a.dtype) for a in (wells, obs_data, obs_var, noise)]
    return pl.pallas_call(
        prepare_kernel,
        out_shape=(edge, edge, jax.ShapeDtypeStruct(log_perm.shape, BF16), full, full, *small),
        in_specs=[pl.BlockSpec(memory_space=pltpu.HBM)] * 6,
        out_specs=[pl.BlockSpec(memory_space=pltpu.VMEM)] * 9,
        scratch_shapes=[
            pltpu.VMEM(log_perm.shape, F32),
            pltpu.VMEM(log_perm.shape, F32),
            pltpu.SemaphoreType.DMA((8,)),
        ],
        cost_estimate=pl.CostEstimate(flops=2_000_000, bytes_accessed=1_600_000, transcendentals=65536),
        compiler_params=pltpu.CompilerParams(vmem_limit_bytes=VMEM_LIMIT),
        name="prepare",
    )(*[pltpu.with_memory_space_constraint(a, pltpu.HBM) for a in (log_perm, conc, wells, obs_data, obs_var, noise)])


def spread_kernel(found_ref, out_ref):
    total = found_ref[0]
    for i in range(1, found_ref.shape[0]):
        total = total + found_ref[i]
    for copy in range(out_ref.shape[0]):
        out_ref[copy] = total


def spread(found, copies):
    return pl.pallas_call(
        spread_kernel,
        out_shape=jax.ShapeDtypeStruct((copies, *found.shape[1:]), found.dtype),
        cost_estimate=pl.CostEstimate(flops=65536, bytes_accessed=400_000, transcendentals=0),
        compiler_params=pltpu.CompilerParams(vmem_limit_bytes=VMEM_LIMIT),
        name="spread",
    )(found)


def advance_kernel(conc_ref, conduct_ref, part_ref, far_ref, near_ref, wells_ref, out_ref, picked_ref):
    strip = lax.axis_index(SPACE)
    conc0, conc1 = conc_ref[0], conc_ref[1]
    cond0, cond1 = conduct_ref[0], conduct_ref[1]
    even = lax.rem(strip, 2) == 0
    near = [near_ref[i].astype(F32) for i in range(3)]
    far = [far_ref[i].astype(F32) for i in range(3)]
    conc_a, cond_a, part_a = [jnp.where(even, f, n) for n, f in zip(near, far)]
    conc_b, cond_b, part_b = [jnp.where(even, n, f) for n, f in zip(near, far)]
    link_a = 0.5 * (cond0 + cond_a)
    link_b = 0.5 * (cond1 + cond_b)
    gain_a = time_step * (link_a * (conc_a - conc0))
    gain_b = time_step * (link_b * (conc_b - conc1))
    once0, once1 = part_ref[0] + gain_a, part_ref[1] + gain_b
    once_a = jnp.where(strip == 0, 0.0, part_a - gain_a)
    once_b = jnp.where(strip == STRIPS - 1, 0.0, part_b - gain_b)
    between = 0.5 * (cond0 + cond1) * (once1 - once0)
    twice0 = once0 + time_step * (
        along_row(once0, link_right(cond0), 0.5 * cond0) + between + link_a * (once_a - once0)
    )
    twice1 = once1 + time_step * (
        along_row(once1, link_right(cond1), 0.5 * cond1) - between + link_b * (once_b - once1)
    )
    out_ref[0], out_ref[1] = twice0, twice1
    members, width = twice0.shape
    chunk = 256
    pieces = jnp.concatenate([*split3(twice0), *split3(twice1)], axis=0)
    cell = wells_ref[...] - 2 * strip * width
    column = jnp.where(cell >= width, cell - width, cell)
    total = jnp.zeros((6 * members, 128), F32)
    for start in range(0, width, chunk):
        here = lax.broadcasted_iota(jnp.int32, (chunk, 128), 0) + start
        chosen = jnp.where(here == column, 1.0, 0.0).astype(BF16)
        total = total + jnp.dot(pieces[:, start : start + chunk], chosen, preferred_element_type=F32)
    upper, lower = [
        total[i : i + members] + total[i + members : i + 2 * members] + total[i + 2 * members : i + 3 * members]
        for i in (0, 3 * members)
    ]
    picked = jnp.where(jnp.broadcast_to(cell, upper.shape) >= width, lower, upper)
    picked = jnp.round(picked * GRAIN).astype(jnp.int32).astype(jnp.int16)
    for copy in range(picked_ref.shape[0]):
        picked_ref[copy] = picked


def advance(conc, conduct, part, far, near, wells, copies):
    vmem = pl.BlockSpec(memory_space=pltpu.VMEM)
    return pl.pallas_call(
        advance_kernel,
        out_shape=(
            jax.ShapeDtypeStruct(conc.shape, F32),
            jax.ShapeDtypeStruct((copies, conc.shape[1], 128), jnp.int16),
        ),
        in_specs=[vmem] * 6,
        out_specs=(vmem, vmem),
        cost_estimate=pl.CostEstimate(flops=60_000_000, bytes_accessed=1_800_000, transcendentals=0),
        compiler_params=pltpu.CompilerParams(vmem_limit_bytes=VMEM_LIMIT),
        name="advance",
    )(conc, conduct, part, far, near, wells)


def solve_kernel(found_ref, noise_ref, data_ref, var_ref, out_ref, pred, work, solved):
    group = lax.axis_index(MEM)
    for position, flip in enumerate(ORDER):
        block = lax.bitwise_xor(group, flip)
        place = 8 * lax.rem(block, 2) + block // 2
        code = found_ref[place].astype(jnp.int32) + found_ref[place + 4].astype(jnp.int32)
        pred[pl.ds(position * 16, 16), :] = code.astype(F32) * (1 / GRAIN)
    centred = weights_of(pred[...], pred[0:16], noise_ref[...], data_ref[...], var_ref[...], work, solved)
    out_ref[...] = centred.astype(BF16)


def solve(found, noise, obs_data, obs_var):
    vmem = pl.BlockSpec(memory_space=pltpu.VMEM)
    return pl.pallas_call(
        solve_kernel,
        out_shape=jax.ShapeDtypeStruct((16, 128), BF16),
        in_specs=[vmem] * 4,
        out_specs=vmem,
        scratch_shapes=[
            pltpu.VMEM((128, 128), F32),
            pltpu.VMEM((128, 384), F32),
            pltpu.VMEM((128, 256), F32),
        ],
        cost_estimate=pl.CostEstimate(flops=50_000_000, bytes_accessed=18_000_000, transcendentals=128),
        compiler_params=pltpu.CompilerParams(vmem_limit_bytes=VMEM_LIMIT),
        name="solve",
    )(found, noise, obs_data, obs_var)


def increment_kernel(weights_ref, perm_ref, *refs):
    *pieces, out_ref = refs
    for row in range(2):
        members = [piece[i, row] for piece in pieces for i in range(piece.shape[0])]
        stacked = jnp.concatenate(members, axis=0)
        out_ref[row] = perm_ref[row] + jnp.dot(weights_ref[...], stacked, preferred_element_type=F32)


def increment(weights, log_perm, pieces):
    return pl.pallas_call(
        increment_kernel,
        out_shape=jax.ShapeDtypeStruct(log_perm.shape, F32),
        cost_estimate=pl.CostEstimate(flops=20_000_000, bytes_accessed=1_700_000, transcendentals=0),
        compiler_params=pltpu.CompilerParams(vmem_limit_bytes=VMEM_LIMIT),
        name="increment",
    )(weights, log_perm, *pieces)


STRIPS = 64
PLANES = [list(range(STRIPS // 2 - 1, -1, -1)), list(range(STRIPS // 2, STRIPS))]


def swapped(value, axis, first, count):
    pairs = [(i, i + 1) for i in range(first, count - 1, 2)]
    return lax.ppermute(value, axis, pairs + [(high, low) for low, high in pairs])


def crossed(value, flip):
    return lax.ppermute(value, "z_lo", [(i, i ^ flip) for i in range(4)])


def local(log_perm, concentration, well_cells, obs_data, obs_var, obs_noise):
    near, far, low, part, conduct, wells, data, var, noise = prepare(
        log_perm, concentration, well_cells[None], obs_data[None], obs_var[None], obs_noise
    )
    far = swapped(far, SPACE, 1, STRIPS)
    near = swapped(near, SPACE, 0, STRIPS)
    tracer, picked = advance(concentration, conduct, part, far, near, wells, 32)
    last, *pair = [crossed(low, flip) for flip in (1, 2, 3)]
    pair = jnp.stack(pair)
    found = lax.all_to_all(picked, SPACE, 0, 0, axis_index_groups=PLANES, tiled=True)
    found = lax.all_to_all(spread(found, 16), ("core", "z_hi", "z_lo"), 0, 0, tiled=True)
    mine = [low[None], pair, last[None]]
    pieces = mine + [swapped(piece, "core", 0, 2) for piece in mine]
    weights = solve(found, noise, data, var)
    updated = increment(weights, log_perm, pieces)
    return (tracer, updated)


def solution(mesh):
    fine = Mesh(mesh.devices.reshape(4, 2, 2, 4, 8), MEM + SPACE)
    return jax.shard_map(
        local,
        mesh=fine,
        in_specs=(P(SPACE, MEM, None), P(SPACE, MEM, None), P(), P(), P(), P(MEM, None)),
        out_specs=(P(SPACE, MEM, None), P(SPACE, MEM, None)),
        check_vma=False,
    )
```

```python
import jax
import jax.numpy as jnp
from jax import lax
from jax.experimental import pallas as pl
from jax.experimental.pallas import tpu as pltpu
from jax.sharding import Mesh, PartitionSpec as P

F32, BF16 = jnp.float32, jnp.bfloat16
time_step = 0.03
inflation = 4.0
HIGH = lax.Precision.HIGHEST
TN = (((0,), (0,)), ((), ()))
PANEL = 32
GRAIN = 32000 / 6
MEM = ("z_lo", "core")
SPACE = ("z_hi", "x", "y")
ORDER = (0, 4, 6, 2, 1, 5, 7, 3)
VMEM_LIMIT = 48 * 1024 * 1024

def split3(x):
    hi = x.astype(BF16)
    rest = x - hi.astype(F32)
    mid = rest.astype(BF16)
    low = (rest - mid.astype(F32)).astype(BF16)
    return hi, mid, low


def factor_panel(rows, base):
    height = rows.shape[0]
    index = lax.broadcasted_iota(jnp.int32, (height, 128), 0)
    lanes = rows.shape[1] // 128
    cols = [jnp.broadcast_to(rows[:, base + c : base + c + 1], (height, 128)) for c in range(height)]
    tiles = [rows[:, t * 128 : (t + 1) * 128] for t in range(lanes)]
    for k in range(height):
        scale = lax.rsqrt(cols[k][k : k + 1, :])
        below = cols[k] * scale
        masked = jnp.where(index > k, below, 0.0)
        for c in range(k + 1, height):
            cols[c] = cols[c] - masked * below[c : c + 1, :]
        for t in range(lanes):
            top = tiles[t][k : k + 1, :] * scale
            tiles[t] = jnp.where(index == k, top, tiles[t] - masked * top)
    return jnp.concatenate(tiles, axis=1)


def weights_of(pred, own, own_noise, obs_data, obs_var, work, solved):
    members = pred.shape[0]
    anomaly = pred - jnp.mean(pred, axis=0, keepdims=True)
    innovation = obs_data + jnp.sqrt(inflation * obs_var) * own_noise - own
    cov = lax.dot_general(anomaly, anomaly, TN, precision=HIGH, preferred_element_type=F32) / (members - 1)
    r = lax.broadcasted_iota(jnp.int32, (128, 128), 0)
    c = lax.broadcasted_iota(jnp.int32, (128, 128), 1)
    cov = cov + jnp.where(r == c, jnp.broadcast_to(inflation * obs_var, (128, 128)), 0.0)
    work[:, 0:128] = cov
    work[:, 128:256] = anomaly.T
    padded = jnp.concatenate([innovation, jnp.zeros((112, 128), F32)], axis=0)
    work[:, 256:384] = padded.T
    for p in range(128 // PANEL):
        u = factor_panel(work[p * PANEL : (p + 1) * PANEL, :], p * PANEL)
        solved[p * PANEL : (p + 1) * PANEL, :] = u[:, 128:384]
        if p < 128 // PANEL - 1:
            h, m, l = split3(u)
            left = jnp.concatenate([h, h, m, h, l, m], axis=0)[:, 0:128]
            right = jnp.concatenate([h, m, h, l, h, m], axis=0)
            update = lax.dot_general(left, right, TN, preferred_element_type=F32)
            work[(p + 1) * PANEL :, :] = work[(p + 1) * PANEL :, :] - update[(p + 1) * PANEL :, :]
    w = lax.dot_general(
        solved[:, 128:256], solved[:, 0:128], TN, precision=HIGH, preferred_element_type=F32
    )[:16] / (members - 1)
    return w - jnp.mean(w, axis=1, keepdims=True)


def along_row(conc, link, left_edge):
    width = conc.shape[1]
    lane = lax.broadcasted_iota(jnp.int32, conc.shape, 1)
    right = jnp.where(lane == width - 1, 0.0, pltpu.roll(conc, width - 1, 1))
    flux = link * (right - conc)
    from_left = jnp.where(lane == 0, left_edge * conc, pltpu.roll(flux, 1, 1))
    return flux - from_left


def link_right(conduct):
    width = conduct.shape[1]
    lane = lax.broadcasted_iota(jnp.int32, conduct.shape, 1)
    return 0.5 * (conduct + jnp.where(lane == width - 1, 0.0, pltpu.roll(conduct, width - 1, 1)))


def prepare_kernel(
    perm_hbm, conc_hbm, wells_hbm, data_hbm, var_hbm, noise_hbm,
    near_ref, far_ref, low_ref, part_ref, conduct_ref, wells_ref, data_ref, var_ref, noise_ref,
    perm_ref, conc_ref, sem,
):
    main = [
        pltpu.make_async_copy(source.at[row], target.at[row], sem.at[2 * i + row])
        for i, (source, target) in enumerate(((perm_hbm, perm_ref), (conc_hbm, conc_ref)))
        for row in range(2)
    ]
    small = [
        pltpu.make_async_copy(source, target, sem.at[4 + i])
        for i, (source, target) in enumerate(
            ((wells_hbm, wells_ref), (data_hbm, data_ref), (var_hbm, var_ref), (noise_hbm, noise_ref))
        )
    ]
    for copy in main + small:
        copy.start()
    for copy in main:
        copy.wait()
    perm0, perm1 = perm_ref[0], perm_ref[1]
    conc0, conc1 = conc_ref[0], conc_ref[1]
    low_ref[0], low_ref[1] = perm0.astype(BF16), perm1.astype(BF16)
    cond0, cond1 = jnp.exp(perm0), jnp.exp(perm1)
    conduct_ref[0], conduct_ref[1] = cond0, cond1
    between = 0.5 * (cond0 + cond1) * (conc1 - conc0)
    part0 = conc0 + time_step * (along_row(conc0, link_right(cond0), 0.5 * cond0) + between)
    part1 = conc1 + time_step * (along_row(conc1, link_right(cond1), 0.5 * cond1) - between)
    part_ref[0], part_ref[1] = part0, part1
    even = lax.rem(lax.axis_index(SPACE), 2) == 0
    for i, (low_edge, high_edge) in enumerate(((conc0, conc1), (cond0, cond1), (part0, part1))):
        near_ref[i] = jnp.where(even, high_edge, low_edge).astype(BF16)
        far_ref[i] = jnp.where(even, low_edge, high_edge).astype(BF16)
    for copy in small:
        copy.wait()


def prepare(log_perm, conc, wells, obs_data, obs_var, noise):
    rows, members, width = log_perm.shape
    edge = jax.ShapeDtypeStruct((3, members, width), BF16)
    full = jax.ShapeDtypeStruct(log_perm.shape, F32)
    small = [jax.ShapeDtypeStruct(a.shape, a.dtype) for a in (wells, obs_data, obs_var, noise)]
    return pl.pallas_call(
        prepare_kernel,
        out_shape=(edge, edge, jax.ShapeDtypeStruct(log_perm.shape, BF16), full, full, *small),
        in_specs=[pl.BlockSpec(memory_space=pltpu.HBM)] * 6,
        out_specs=[pl.BlockSpec(memory_space=pltpu.VMEM)] * 9,
        scratch_shapes=[
            pltpu.VMEM(log_perm.shape, F32),
            pltpu.VMEM(log_perm.shape, F32),
            pltpu.SemaphoreType.DMA((8,)),
        ],
        cost_estimate=pl.CostEstimate(flops=2_000_000, bytes_accessed=1_600_000, transcendentals=65536),
        compiler_params=pltpu.CompilerParams(vmem_limit_bytes=VMEM_LIMIT),
        name="prepare",
    )(*[pltpu.with_memory_space_constraint(a, pltpu.HBM) for a in (log_perm, conc, wells, obs_data, obs_var, noise)])


def spread_kernel(found_ref, out_ref):
    total = found_ref[0]
    for i in range(1, found_ref.shape[0]):
        total = total + found_ref[i]
    for copy in range(out_ref.shape[0]):
        out_ref[copy] = total


def spread(found, copies):
    return pl.pallas_call(
        spread_kernel,
        out_shape=jax.ShapeDtypeStruct((copies, *found.shape[1:]), found.dtype),
        cost_estimate=pl.CostEstimate(flops=65536, bytes_accessed=400_000, transcendentals=0),
        compiler_params=pltpu.CompilerParams(vmem_limit_bytes=VMEM_LIMIT),
        name="spread",
    )(found)


def advance_kernel(conc_ref, conduct_ref, part_ref, far_ref, near_ref, wells_ref, out_ref, picked_ref):
    strip = lax.axis_index(SPACE)
    conc0, conc1 = conc_ref[0], conc_ref[1]
    cond0, cond1 = conduct_ref[0], conduct_ref[1]
    even = lax.rem(strip, 2) == 0
    near = [near_ref[i].astype(F32) for i in range(3)]
    far = [far_ref[i].astype(F32) for i in range(3)]
    conc_a, cond_a, part_a = [jnp.where(even, f, n) for n, f in zip(near, far)]
    conc_b, cond_b, part_b = [jnp.where(even, n, f) for n, f in zip(near, far)]
    link_a = 0.5 * (cond0 + cond_a)
    link_b = 0.5 * (cond1 + cond_b)
    gain_a = time_step * (link_a * (conc_a - conc0))
    gain_b = time_step * (link_b * (conc_b - conc1))
    once0, once1 = part_ref[0] + gain_a, part_ref[1] + gain_b
    once_a = jnp.where(strip == 0, 0.0, part_a - gain_a)
    once_b = jnp.where(strip == STRIPS - 1, 0.0, part_b - gain_b)
    between = 0.5 * (cond0 + cond1) * (once1 - once0)
    twice0 = once0 + time_step * (
        along_row(once0, link_right(cond0), 0.5 * cond0) + between + link_a * (once_a - once0)
    )
    twice1 = once1 + time_step * (
        along_row(once1, link_right(cond1), 0.5 * cond1) - between + link_b * (once_b - once1)
    )
    out_ref[0], out_ref[1] = twice0, twice1
    members, width = twice0.shape
    chunk = 256
    pieces = jnp.concatenate([*split3(twice0), *split3(twice1)], axis=0)
    cell = wells_ref[...] - 2 * strip * width
    column = jnp.where(cell >= width, cell - width, cell)
    total = jnp.zeros((6 * members, 128), F32)
    for start in range(0, width, chunk):
        here = lax.broadcasted_iota(jnp.int32, (chunk, 128), 0) + start
        chosen = jnp.where(here == column, 1.0, 0.0).astype(BF16)
        total = total + jnp.dot(pieces[:, start : start + chunk], chosen, preferred_element_type=F32)
    upper, lower = [
        total[i : i + members] + total[i + members : i + 2 * members] + total[i + 2 * members : i + 3 * members]
        for i in (0, 3 * members)
    ]
    picked = jnp.where(jnp.broadcast_to(cell, upper.shape) >= width, lower, upper)
    picked = jnp.round(picked * GRAIN).astype(jnp.int32).astype(jnp.int16)
    for copy in range(picked_ref.shape[0]):
        picked_ref[copy] = picked


def advance(conc, conduct, part, far, near, wells, copies):
    vmem = pl.BlockSpec(memory_space=pltpu.VMEM)
    return pl.pallas_call(
        advance_kernel,
        out_shape=(
            jax.ShapeDtypeStruct(conc.shape, F32),
            jax.ShapeDtypeStruct((copies, conc.shape[1], 128), jnp.int16),
        ),
        in_specs=[vmem] * 6,
        out_specs=(vmem, vmem),
        cost_estimate=pl.CostEstimate(flops=60_000_000, bytes_accessed=1_800_000, transcendentals=0),
        compiler_params=pltpu.CompilerParams(vmem_limit_bytes=VMEM_LIMIT),
        name="advance",
    )(conc, conduct, part, far, near, wells)


def solve_kernel(found_ref, noise_ref, data_ref, var_ref, out_ref, pred, work, solved):
    group = lax.axis_index(MEM)
    for position, flip in enumerate(ORDER):
        block = lax.bitwise_xor(group, flip)
        place = 4 * lax.rem(block, 2) + block // 2
        code = found_ref[place].astype(jnp.int32) + found_ref[place + 8].astype(jnp.int32)
        pred[pl.ds(position * 16, 16), :] = code.astype(F32) * (1 / GRAIN)
    centred = weights_of(pred[...], pred[0:16], noise_ref[...], data_ref[...], var_ref[...], work, solved)
    out_ref[...] = centred.astype(BF16)


def solve(found, noise, obs_data, obs_var):
    vmem = pl.BlockSpec(memory_space=pltpu.VMEM)
    return pl.pallas_call(
        solve_kernel,
        out_shape=jax.ShapeDtypeStruct((16, 128), BF16),
        in_specs=[vmem] * 4,
        out_specs=vmem,
        scratch_shapes=[
            pltpu.VMEM((128, 128), F32),
            pltpu.VMEM((128, 384), F32),
            pltpu.VMEM((128, 256), F32),
        ],
        cost_estimate=pl.CostEstimate(flops=50_000_000, bytes_accessed=18_000_000, transcendentals=128),
        compiler_params=pltpu.CompilerParams(vmem_limit_bytes=VMEM_LIMIT),
        name="solve",
    )(found, noise, obs_data, obs_var)


def increment_kernel(weights_ref, perm_ref, *refs):
    *pieces, out_ref = refs
    for row in range(2):
        members = [piece[i, row] for piece in pieces for i in range(piece.shape[0])]
        stacked = jnp.concatenate(members, axis=0)
        out_ref[row] = perm_ref[row] + jnp.dot(weights_ref[...], stacked, preferred_element_type=F32)


def increment(weights, log_perm, pieces):
    return pl.pallas_call(
        increment_kernel,
        out_shape=jax.ShapeDtypeStruct(log_perm.shape, F32),
        cost_estimate=pl.CostEstimate(flops=20_000_000, bytes_accessed=1_700_000, transcendentals=0),
        compiler_params=pltpu.CompilerParams(vmem_limit_bytes=VMEM_LIMIT),
        name="increment",
    )(weights, log_perm, *pieces)


STRIPS = 64
COLUMNS = [
    [128 * z + 64 * core + 32 * half + column for half in (1, 0) for core in (0, 1) for z in range(4)]
    for column in range(STRIPS // 2)
]
PLANES = [list(range(STRIPS // 2 - 1, -1, -1)), list(range(STRIPS // 2, STRIPS))]


def swapped(value, axis, first, count):
    pairs = [(i, i + 1) for i in range(first, count - 1, 2)]
    return lax.ppermute(value, axis, pairs + [(high, low) for low, high in pairs])


def crossed(value, flip):
    return lax.ppermute(value, "z_lo", [(i, i ^ flip) for i in range(4)])


def local(log_perm, concentration, well_cells, obs_data, obs_var, obs_noise):
    near, far, low, part, conduct, wells, data, var, noise = prepare(
        log_perm, concentration, well_cells[None], obs_data[None], obs_var[None], obs_noise
    )
    far = swapped(far, SPACE, 1, STRIPS)
    near = swapped(near, SPACE, 0, STRIPS)
    tracer, picked = advance(concentration, conduct, part, far, near, wells, 32)
    last, *pair = [crossed(low, flip) for flip in (1, 2, 3)]
    pair = jnp.stack(pair)
    found = lax.all_to_all(picked, SPACE, 0, 0, axis_index_groups=PLANES, tiled=True)
    found = lax.all_to_all(spread(found, 16), MEM + SPACE, 0, 0, axis_index_groups=COLUMNS, tiled=True)
    mine = [low[None], pair, last[None]]
    pieces = mine + [swapped(piece, "core", 0, 2) for piece in mine]
    weights = solve(found, noise, data, var)
    updated = increment(weights, log_perm, pieces)
    return (tracer, updated)


def solution(mesh):
    fine = Mesh(mesh.devices.reshape(4, 2, 2, 4, 8), MEM + SPACE)
    return jax.shard_map(
        local,
        mesh=fine,
        in_specs=(P(SPACE, MEM, None), P(SPACE, MEM, None), P(), P(), P(), P(MEM, None)),
        out_specs=(P(SPACE, MEM, None), P(SPACE, MEM, None)),
        check_vma=False,
    )
```

```python
import jax
import jax.numpy as jnp
from jax import lax
from jax.experimental import pallas as pl
from jax.experimental.pallas import tpu as pltpu
from jax.sharding import Mesh, PartitionSpec as P

F32, BF16 = jnp.float32, jnp.bfloat16
time_step = 0.03
inflation = 4.0
HIGH = lax.Precision.HIGHEST
TN = (((0,), (0,)), ((), ()))
PANEL = 32
GRAIN = 32000 / 6
MEM = ("z_lo", "core")
SPACE = ("z_hi", "x", "y")
ORDER = (0, 2, 4, 6, 1, 3, 5, 7)
VMEM_LIMIT = 48 * 1024 * 1024

def split3(x):
    hi = x.astype(BF16)
    rest = x - hi.astype(F32)
    mid = rest.astype(BF16)
    low = (rest - mid.astype(F32)).astype(BF16)
    return hi, mid, low


def factor_panel(rows, base):
    height = rows.shape[0]
    index = lax.broadcasted_iota(jnp.int32, (height, 128), 0)
    lanes = rows.shape[1] // 128
    cols = [jnp.broadcast_to(rows[:, base + c : base + c + 1], (height, 128)) for c in range(height)]
    tiles = [rows[:, t * 128 : (t + 1) * 128] for t in range(lanes)]
    for k in range(height):
        scale = lax.rsqrt(cols[k][k : k + 1, :])
        below = cols[k] * scale
        masked = jnp.where(index > k, below, 0.0)
        for c in range(k + 1, height):
            cols[c] = cols[c] - masked * below[c : c + 1, :]
        for t in range(lanes):
            top = tiles[t][k : k + 1, :] * scale
            tiles[t] = jnp.where(index == k, top, tiles[t] - masked * top)
    return jnp.concatenate(tiles, axis=1)


def weights_of(pred, own, own_noise, obs_data, obs_var, work, solved):
    members = pred.shape[0]
    anomaly = pred - jnp.mean(pred, axis=0, keepdims=True)
    innovation = obs_data + jnp.sqrt(inflation * obs_var) * own_noise - own
    cov = lax.dot_general(anomaly, anomaly, TN, precision=HIGH, preferred_element_type=F32) / (members - 1)
    r = lax.broadcasted_iota(jnp.int32, (128, 128), 0)
    c = lax.broadcasted_iota(jnp.int32, (128, 128), 1)
    cov = cov + jnp.where(r == c, jnp.broadcast_to(inflation * obs_var, (128, 128)), 0.0)
    work[:, 0:128] = cov
    work[:, 128:256] = anomaly.T
    padded = jnp.concatenate([innovation, jnp.zeros((112, 128), F32)], axis=0)
    work[:, 256:384] = padded.T
    for p in range(128 // PANEL):
        u = factor_panel(work[p * PANEL : (p + 1) * PANEL, :], p * PANEL)
        solved[p * PANEL : (p + 1) * PANEL, :] = u[:, 128:384]
        if p < 128 // PANEL - 1:
            h, m, l = split3(u)
            left = jnp.concatenate([h, h, m, h, l, m], axis=0)[:, 0:128]
            right = jnp.concatenate([h, m, h, l, h, m], axis=0)
            update = lax.dot_general(left, right, TN, preferred_element_type=F32)
            work[(p + 1) * PANEL :, :] = work[(p + 1) * PANEL :, :] - update[(p + 1) * PANEL :, :]
    w = lax.dot_general(
        solved[:, 128:256], solved[:, 0:128], TN, precision=HIGH, preferred_element_type=F32
    )[:16] / (members - 1)
    return w - jnp.mean(w, axis=1, keepdims=True)


def along_row(conc, link, left_edge):
    width = conc.shape[1]
    lane = lax.broadcasted_iota(jnp.int32, conc.shape, 1)
    right = jnp.where(lane == width - 1, 0.0, pltpu.roll(conc, width - 1, 1))
    flux = link * (right - conc)
    from_left = jnp.where(lane == 0, left_edge * conc, pltpu.roll(flux, 1, 1))
    return flux - from_left


def link_right(conduct):
    width = conduct.shape[1]
    lane = lax.broadcasted_iota(jnp.int32, conduct.shape, 1)
    return 0.5 * (conduct + jnp.where(lane == width - 1, 0.0, pltpu.roll(conduct, width - 1, 1)))


def prepare_kernel(
    perm_hbm, conc_hbm, wells_hbm, data_hbm, var_hbm, noise_hbm,
    near_ref, far_ref, low_ref, part_ref, conduct_ref, wells_ref, data_ref, var_ref, noise_ref,
    perm_ref, conc_ref, sem,
):
    main = [
        pltpu.make_async_copy(source.at[row], target.at[row], sem.at[2 * i + row])
        for i, (source, target) in enumerate(((perm_hbm, perm_ref), (conc_hbm, conc_ref)))
        for row in range(2)
    ]
    small = [
        pltpu.make_async_copy(source, target, sem.at[4 + i])
        for i, (source, target) in enumerate(
            ((wells_hbm, wells_ref), (data_hbm, data_ref), (var_hbm, var_ref), (noise_hbm, noise_ref))
        )
    ]
    for copy in main + small:
        copy.start()
    for copy in main:
        copy.wait()
    perm0, perm1 = perm_ref[0], perm_ref[1]
    conc0, conc1 = conc_ref[0], conc_ref[1]
    low_ref[0], low_ref[1] = perm0.astype(BF16), perm1.astype(BF16)
    cond0, cond1 = jnp.exp(perm0), jnp.exp(perm1)
    conduct_ref[0], conduct_ref[1] = cond0, cond1
    between = 0.5 * (cond0 + cond1) * (conc1 - conc0)
    part0 = conc0 + time_step * (along_row(conc0, link_right(cond0), 0.5 * cond0) + between)
    part1 = conc1 + time_step * (along_row(conc1, link_right(cond1), 0.5 * cond1) - between)
    part_ref[0], part_ref[1] = part0, part1
    even = lax.rem(lax.axis_index(SPACE), 2) == 0
    for i, (low_edge, high_edge) in enumerate(((conc0, conc1), (cond0, cond1), (part0, part1))):
        near_ref[i] = jnp.where(even, high_edge, low_edge).astype(BF16)
        far_ref[i] = jnp.where(even, low_edge, high_edge).astype(BF16)
    for copy in small:
        copy.wait()


def prepare(log_perm, conc, wells, obs_data, obs_var, noise):
    rows, members, width = log_perm.shape
    edge = jax.ShapeDtypeStruct((3, members, width), BF16)
    full = jax.ShapeDtypeStruct(log_perm.shape, F32)
    small = [jax.ShapeDtypeStruct(a.shape, a.dtype) for a in (wells, obs_data, obs_var, noise)]
    return pl.pallas_call(
        prepare_kernel,
        out_shape=(edge, edge, jax.ShapeDtypeStruct(log_perm.shape, BF16), full, full, *small),
        in_specs=[pl.BlockSpec(memory_space=pltpu.HBM)] * 6,
        out_specs=[pl.BlockSpec(memory_space=pltpu.VMEM)] * 9,
        scratch_shapes=[
            pltpu.VMEM(log_perm.shape, F32),
            pltpu.VMEM(log_perm.shape, F32),
            pltpu.SemaphoreType.DMA((8,)),
        ],
        cost_estimate=pl.CostEstimate(flops=2_000_000, bytes_accessed=1_600_000, transcendentals=65536),
        compiler_params=pltpu.CompilerParams(vmem_limit_bytes=VMEM_LIMIT),
        name="prepare",
    )(*[pltpu.with_memory_space_constraint(a, pltpu.HBM) for a in (log_perm, conc, wells, obs_data, obs_var, noise)])


def spread_kernel(found_ref, out_ref):
    total = found_ref[0]
    for i in range(1, found_ref.shape[0]):
        total = total + found_ref[i]
    for copy in range(out_ref.shape[0]):
        out_ref[copy] = total


def spread(found, copies):
    return pl.pallas_call(
        spread_kernel,
        out_shape=jax.ShapeDtypeStruct((copies, *found.shape[1:]), found.dtype),
        cost_estimate=pl.CostEstimate(flops=65536, bytes_accessed=400_000, transcendentals=0),
        compiler_params=pltpu.CompilerParams(vmem_limit_bytes=VMEM_LIMIT),
        name="spread",
    )(found)


def advance_kernel(conc_ref, conduct_ref, part_ref, far_ref, near_ref, wells_ref, out_ref, picked_ref):
    strip = lax.axis_index(SPACE)
    conc0, conc1 = conc_ref[0], conc_ref[1]
    cond0, cond1 = conduct_ref[0], conduct_ref[1]
    even = lax.rem(strip, 2) == 0
    near = [near_ref[i].astype(F32) for i in range(3)]
    far = [far_ref[i].astype(F32) for i in range(3)]
    conc_a, cond_a, part_a = [jnp.where(even, f, n) for n, f in zip(near, far)]
    conc_b, cond_b, part_b = [jnp.where(even, n, f) for n, f in zip(near, far)]
    link_a = 0.5 * (cond0 + cond_a)
    link_b = 0.5 * (cond1 + cond_b)
    gain_a = time_step * (link_a * (conc_a - conc0))
    gain_b = time_step * (link_b * (conc_b - conc1))
    once0, once1 = part_ref[0] + gain_a, part_ref[1] + gain_b
    once_a = jnp.where(strip == 0, 0.0, part_a - gain_a)
    once_b = jnp.where(strip == STRIPS - 1, 0.0, part_b - gain_b)
    between = 0.5 * (cond0 + cond1) * (once1 - once0)
    twice0 = once0 + time_step * (
        along_row(once0, link_right(cond0), 0.5 * cond0) + between + link_a * (once_a - once0)
    )
    twice1 = once1 + time_step * (
        along_row(once1, link_right(cond1), 0.5 * cond1) - between + link_b * (once_b - once1)
    )
    out_ref[0], out_ref[1] = twice0, twice1
    members, width = twice0.shape
    chunk = 256
    pieces = jnp.concatenate([*split3(twice0), *split3(twice1)], axis=0)
    cell = wells_ref[...] - 2 * strip * width
    column = jnp.where(cell >= width, cell - width, cell)
    total = jnp.zeros((6 * members, 128), F32)
    for start in range(0, width, chunk):
        here = lax.broadcasted_iota(jnp.int32, (chunk, 128), 0) + start
        chosen = jnp.where(here == column, 1.0, 0.0).astype(BF16)
        total = total + jnp.dot(pieces[:, start : start + chunk], chosen, preferred_element_type=F32)
    upper, lower = [
        total[i : i + members] + total[i + members : i + 2 * members] + total[i + 2 * members : i + 3 * members]
        for i in (0, 3 * members)
    ]
    picked = jnp.where(jnp.broadcast_to(cell, upper.shape) >= width, lower, upper)
    picked = jnp.round(picked * GRAIN).astype(jnp.int32).astype(jnp.int16)
    for copy in range(picked_ref.shape[0]):
        picked_ref[copy] = picked


def advance(conc, conduct, part, far, near, wells, copies):
    vmem = pl.BlockSpec(memory_space=pltpu.VMEM)
    return pl.pallas_call(
        advance_kernel,
        out_shape=(
            jax.ShapeDtypeStruct(conc.shape, F32),
            jax.ShapeDtypeStruct((copies, conc.shape[1], 128), jnp.int16),
        ),
        in_specs=[vmem] * 6,
        out_specs=(vmem, vmem),
        cost_estimate=pl.CostEstimate(flops=60_000_000, bytes_accessed=1_800_000, transcendentals=0),
        compiler_params=pltpu.CompilerParams(vmem_limit_bytes=VMEM_LIMIT),
        name="advance",
    )(conc, conduct, part, far, near, wells)


def solve_kernel(found_ref, noise_ref, data_ref, var_ref, out_ref, pred, work, solved):
    group = lax.axis_index(MEM)
    for position, flip in enumerate(ORDER):
        block = lax.bitwise_xor(group, flip)
        place = 4 * lax.rem(block, 2) + block // 2
        code = found_ref[place].astype(jnp.int32) + found_ref[place + 8].astype(jnp.int32)
        pred[pl.ds(position * 16, 16), :] = code.astype(F32) * (1 / GRAIN)
    centred = weights_of(pred[...], pred[0:16], noise_ref[...], data_ref[...], var_ref[...], work, solved)
    out_ref[...] = centred.astype(BF16)


def solve(found, noise, obs_data, obs_var):
    vmem = pl.BlockSpec(memory_space=pltpu.VMEM)
    return pl.pallas_call(
        solve_kernel,
        out_shape=jax.ShapeDtypeStruct((16, 128), BF16),
        in_specs=[vmem] * 4,
        out_specs=vmem,
        scratch_shapes=[
            pltpu.VMEM((128, 128), F32),
            pltpu.VMEM((128, 384), F32),
            pltpu.VMEM((128, 256), F32),
        ],
        cost_estimate=pl.CostEstimate(flops=50_000_000, bytes_accessed=18_000_000, transcendentals=128),
        compiler_params=pltpu.CompilerParams(vmem_limit_bytes=VMEM_LIMIT),
        name="solve",
    )(found, noise, obs_data, obs_var)


def increment_kernel(weights_ref, perm_ref, *refs):
    *pieces, out_ref = refs
    for row in range(2):
        members = [piece[i, row] for piece in pieces for i in range(piece.shape[0])]
        stacked = jnp.concatenate(members, axis=0)
        out_ref[row] = perm_ref[row] + jnp.dot(weights_ref[...], stacked, preferred_element_type=F32)


def increment(weights, log_perm, pieces):
    return pl.pallas_call(
        increment_kernel,
        out_shape=jax.ShapeDtypeStruct(log_perm.shape, F32),
        cost_estimate=pl.CostEstimate(flops=20_000_000, bytes_accessed=1_700_000, transcendentals=0),
        compiler_params=pltpu.CompilerParams(vmem_limit_bytes=VMEM_LIMIT),
        name="increment",
    )(weights, log_perm, *pieces)


STRIPS = 64
COLUMNS = [
    [128 * z + 64 * core + 32 * half + column for half in (1, 0) for core in (0, 1) for z in range(4)]
    for column in range(STRIPS // 2)
]
PLANES = [list(range(STRIPS // 2 - 1, -1, -1)), list(range(STRIPS // 2, STRIPS))]


def swapped(value, axis, first, count):
    pairs = [(i, i + 1) for i in range(first, count - 1, 2)]
    return lax.ppermute(value, axis, pairs + [(high, low) for low, high in pairs])


def crossed(value, flip):
    return lax.ppermute(value, "z_lo", [(i, i ^ flip) for i in range(4)])


def local(log_perm, concentration, well_cells, obs_data, obs_var, obs_noise):
    near, far, low, part, conduct, wells, data, var, noise = prepare(
        log_perm, concentration, well_cells[None], obs_data[None], obs_var[None], obs_noise
    )
    far = swapped(far, SPACE, 1, STRIPS)
    near = swapped(near, SPACE, 0, STRIPS)
    tracer, picked = advance(concentration, conduct, part, far, near, wells, 32)
    last, *pair = [crossed(low, flip) for flip in (3, 1, 2)]
    pair = jnp.stack(pair)
    found = lax.all_to_all(picked, SPACE, 0, 0, axis_index_groups=PLANES, tiled=True)
    found = lax.all_to_all(spread(found, 16), MEM + SPACE, 0, 0, axis_index_groups=COLUMNS, tiled=True)
    mine = [low[None], pair, last[None]]
    pieces = mine + [swapped(piece, "core", 0, 2) for piece in mine]
    weights = solve(found, noise, data, var)
    updated = increment(weights, log_perm, pieces)
    return (tracer, updated)


def solution(mesh):
    fine = Mesh(mesh.devices.reshape(4, 2, 2, 4, 8), MEM + SPACE)
    return jax.shard_map(
        local,
        mesh=fine,
        in_specs=(P(SPACE, MEM, None), P(SPACE, MEM, None), P(), P(), P(), P(MEM, None)),
        out_specs=(P(SPACE, MEM, None), P(SPACE, MEM, None)),
        check_vma=False,
    )
```
